256 devices in a mesh: pair: 2 (over y_hi), tm: 128 (over y_lo, x, z, core).
Axes of the slice: x: 4, y: 4 (y_hi: 2, y_lo: 2; y = y_hi * 2 + y_lo), z: 8, core: 2. Of those that a mesh axis runs over, the one named last changes fastest.
Arguments:
- fields: float32 [2, 128, 256, 256], P('pair', 'tm'), may hold values from -4 to 4
- forcing: float32 [2, 128, 256, 256], P('pair', 'tm'), may hold values from -4 to 4.3
- diffusion: float32 [256, 256], replicated, may hold values from 0.5 to 2
- reaction: float32 [256, 256], replicated, may hold values from 0.02 to 0.2
- wrap_factor: float32 [1], replicated, may hold values from 0.05 to 0.4
- mean_diffusion: float32 [1], replicated, may hold values from 0.8 to 1.25
- spectral_shift: float32 [1], replicated, may hold values from 0.05 to 1
Outputs:
- updated: float32 [2, 128, 256, 256], P('pair', 'tm')
The draws below stay inside these ranges and needn't reach their ends.
All inputs are finite; a program needn't handle non-finite values.
Results may differ from the reference program's by a relative error of at most 0.0003.
Values sent between devices are 32-bit elements; how exact they have to be, the bound alone decides.
A program may use at most 64 MiB of HBM per device.

```python
import math
import jax
import jax.numpy as jnp
from jax import lax

NX = 256
NY = 256
ITERS = 2
NT = 128


def draw_forcing(key, part):
    base = jnp.clip(jax.random.normal(key, (2, NT, NX, NY), jnp.float32), -4.0, 4.0)
    return base


def steps_of(rng, shape, pieces, least, high):
    def one(dim, blocks):
        heights = jax.random.uniform(jax.random.fold_in(jax.random.fold_in(rng, 6), dim), (blocks,), jnp.float32, least / len(pieces), high / len(pieces))
        return jnp.repeat(jnp.exp(heights), shape[dim] // blocks).reshape((-1,) + (1,) * (len(shape) - dim - 1))

    loudness = one(*pieces[0])
    for cut in pieces[1:]:
        loudness = loudness * one(*cut)
    return loudness


def bell_draw(own_key, extent, deviation, reach, split=(), kind=jnp.bfloat16):
    entries = jax.random.normal(own_key, extent, jnp.float32) * deviation
    if len(split) > 0:
        entries = steps_of(own_key, extent, split, -0.22, 0.18) * entries
    return jnp.clip(entries, min=-reach, max=reach).astype(kind)


def setup_inputs(seed: int = 0) -> dict:
    seeds = jax.random.split(jax.random.key(seed), 8)
    fields = bell_draw(seeds[0], (2, NT, NX, NY), 1.0, 4.0, ((0, 2), (1, 128)), jnp.float32)
    forcing = draw_forcing(jax.random.fold_in(seeds[7], 71), 0)
    diffusion = jnp.clip(jnp.exp(jax.random.uniform(seeds[2], (NX, NY), jnp.float32, math.log(0.5), math.log(2.0))), 0.5, 2.0)
    reaction = jnp.clip(jnp.exp(jax.random.uniform(seeds[3], (NX, NY), jnp.float32, math.log(0.02), math.log(0.2))), 0.02, 0.2)
    wrap_factor = jnp.clip(jax.random.uniform(seeds[4], (1,), jnp.float32, 0.05, 0.4), 0.05, 0.4)
    mean_diffusion = jnp.clip(jax.random.uniform(seeds[5], (1,), jnp.float32, 0.8, 1.25), 0.8, 1.25)
    spectral_shift = jnp.clip(jnp.exp(jax.random.uniform(seeds[6], (1,), jnp.float32, math.log(0.05), math.log(1.0))), 0.05, 1.0)
    return {"fields": fields, "forcing": forcing, "diffusion": diffusion, "reaction": reaction, "wrap_factor": wrap_factor, "mean_diffusion": mean_diffusion, "spectral_shift": spectral_shift}


gamma_inv = 0.5
step_rate = 1.0


def face_weights(diffusion):
    east_face = 0.5 * (diffusion + jnp.roll(diffusion, -1, 0))
    north_face = 0.5 * (diffusion + jnp.roll(diffusion, -1, 1))
    return east_face, north_face


def transport(values, east_face, north_face):
    flux_x = east_face * (jnp.roll(values, -1, -2) - values)
    flux_y = north_face * (jnp.roll(values, -1, -1) - values)
    return flux_x - jnp.roll(flux_x, 1, -2) + flux_y - jnp.roll(flux_y, 1, -1)


def residual_terms(own_field, earlier, partner, source, spread, reaction, adjoint_flag):
    state_coupling = reaction * own_field * own_field * own_field + gamma_inv * partner
    adjoint_coupling = 3.0 * reaction * partner * partner * own_field - partner
    coupling = jnp.where(adjoint_flag, adjoint_coupling, state_coupling)
    return source - ((own_field - earlier) * step_rate - spread + coupling)


def time_parts(mode_ids, total, log_alpha):
    ratio = jnp.exp(log_alpha / total)
    angles = (mode_ids % total).astype(jnp.float32) * (2.0 * math.pi / total)
    return step_rate * (1.0 - ratio * jnp.cos(angles)), step_rate * ratio * jnp.sin(angles)


def space_eigen(row_ids, col_ids, width_x, width_y):
    sine_rows = jnp.sin(row_ids.astype(jnp.float32) * (math.pi / width_x))
    sine_cols = jnp.sin(col_ids.astype(jnp.float32) * (math.pi / width_y))
    return 4.0 * sine_rows[:, None] ** 2 + 4.0 * sine_cols[None, :] ** 2


def reference(fields, forcing, diffusion, reaction, wrap_factor, mean_diffusion, spectral_shift):
    east_face, north_face = face_weights(diffusion)
    log_alpha = jnp.log(wrap_factor[0])
    time_ids = jnp.arange(NT, dtype=jnp.int32)
    time_scale = jnp.exp(time_ids.astype(jnp.float32) * (log_alpha / NT))
    time_re, time_im = time_parts(time_ids, NT, log_alpha)
    eigenvalue = space_eigen(jnp.arange(NX, dtype=jnp.int32), jnp.arange(NY, dtype=jnp.int32), NX, NY)
    den_re = time_re[:, None, None] + (mean_diffusion[0] * eigenvalue + spectral_shift[0])
    den_im = jnp.broadcast_to(time_im[:, None, None], den_re.shape)
    divisor = lax.complex(den_re, den_im)
    state_field = fields[0]
    adjoint = fields[1]
    zero_step = jnp.zeros((1, NX, NY), jnp.float32)
    for iteration in range(ITERS):
        new_pair = []
        for group_id, members in enumerate(((state_field, adjoint), (adjoint, state_field))):
            own_field, other_field = members
            if group_id == 0:
                earlier = jnp.concatenate([zero_step, own_field[:-1]], 0)
            else:
                earlier = jnp.concatenate([own_field[1:], zero_step], 0)
            spread = transport(own_field, east_face, north_face)
            residual = residual_terms(own_field, earlier, other_field, forcing[group_id], spread, reaction, group_id == 1)
            if group_id == 1:
                residual = jnp.flip(residual, 0)
            spectrum = jnp.fft.fftn(residual * time_scale[:, None, None])
            correction = jnp.fft.ifftn(spectrum / divisor).real / time_scale[:, None, None]
            if group_id == 1:
                correction = jnp.flip(correction, 0)
            new_pair.append(own_field + correction)
        state_field, adjoint = new_pair
    return jnp.stack([state_field, adjoint])
```

```python
import math

import jax
import jax.numpy as jnp
import numpy as np
from jax import lax
from jax.sharding import PartitionSpec as P

ITERS = 2
GAMMA_INV = 0.5


def cas_matrix(length):
    wrapped = np.outer(np.arange(length), np.arange(length)) % length
    angles = wrapped * (2.0 * math.pi / length)
    return ((np.cos(angles) + np.sin(angles)) / math.sqrt(length)).astype(np.float32)


def both_sides(matrix, values):
    left = jnp.dot(values, matrix, precision=lax.Precision.HIGH)
    return jnp.dot(matrix, left, precision=lax.Precision.HIGH)


def spread_of(values, face_x, face_y):
    flux_x = face_x * (jnp.roll(values, -1, 0) - values)
    flux_y = face_y * (jnp.roll(values, -1, 1) - values)
    return flux_x - jnp.roll(flux_x, 1, 0) + flux_y - jnp.roll(flux_y, 1, 1)


def time_sweep(rhs, ratio, alpha, last):
    steps = rhs.shape[0]
    part = ratio * rhs
    power = ratio
    width = 1
    while width < steps:
        moved = jnp.concatenate([jnp.zeros_like(part[:width]), part[:-width]], 0)
        part = part + power * moved
        power = power * power
        width *= 2
    carry = alpha * (part[-1:] - last) / (1.0 - alpha * power)
    ages = jnp.arange(1, steps + 1, dtype=jnp.float32)[:, None]
    decay = jnp.exp(ages * jnp.log(ratio))
    return part + decay * carry


def on_device(fields, forcing, diffusion, reaction, wrap_factor, mean_diffusion, spectral_shift):
    place = lax.axis_index("tm")
    count = lax.axis_size("tm")
    adjoint = lax.axis_index("pair") == 1
    values = fields[0, 0]
    source = forcing[0, 0]
    size = values.shape[0]
    alpha = wrap_factor[0]
    mean = mean_diffusion[0]
    shift = spectral_shift[0]
    face_x = 0.5 * (diffusion + jnp.roll(diffusion, -1, 0)) - mean
    face_y = 0.5 * (diffusion + jnp.roll(diffusion, -1, 1)) - mean
    matrix = jnp.asarray(cas_matrix(size))
    sines = jnp.sin(jnp.arange(size, dtype=jnp.float32) * (math.pi / size)) ** 2
    rows = size // count
    own = lax.dynamic_slice_in_dim(sines, place * rows, rows)
    eigen = 4.0 * own[:, None] + 4.0 * sines[None, :]
    ratio = (1.0 / (1.0 + mean * eigen + shift)).reshape(1, rows * size)
    ends = [(count - 1, 0), (count, 2 * count - 1)]
    wrapped = lax.ppermute(values, ("pair", "tm"), ends)
    last = jnp.zeros_like(ratio)

    for _ in range(ITERS):
        partner = lax.ppermute(values, "pair", [(0, 1), (1, 0)])
        state = reaction * values * values * values + GAMMA_INV * partner
        dual = 3.0 * reaction * partner * partner * values - partner
        coupling = jnp.where(adjoint, dual, state)
        rhs = source + shift * values + spread_of(values, face_x, face_y) - coupling
        rhs = rhs - alpha * wrapped
        modes = both_sides(matrix, rhs).reshape(count, rows * size)
        times = lax.all_to_all(modes, "tm", split_axis=0, concat_axis=0, tiled=True)
        times = jnp.where(adjoint, jnp.flip(times, 0), times)
        times = time_sweep(times, ratio, alpha, last)
        last = times[-1:]
        wrapped = jnp.zeros_like(values)
        times = jnp.where(adjoint, jnp.flip(times, 0), times)
        modes = lax.all_to_all(times, "tm", split_axis=0, concat_axis=0, tiled=True)
        values = both_sides(matrix, modes.reshape(size, size))
    return values[None, None]


def solution(mesh):
    split = P("pair", "tm", None, None)
    return jax.shard_map(
        on_device,
        mesh=mesh,
        in_specs=(split, split, P(), P(), P(), P(), P()),
        out_specs=split,
        check_vma=False,
    )
```

```python
import math

import jax
import jax.numpy as jnp
import numpy as np
from jax import lax
from jax.experimental import pallas as pl
from jax.experimental.pallas import tpu as pltpu
from jax.sharding import PartitionSpec as P

ITERS = 2
GAMMA_INV = 0.5
SIZE = 256
STEPS = 128
SUB = 4
LANES = 128
RUN = 16
MESH = pl.DeviceIdType.MESH


def cas_matrix(length):
    wrapped = np.outer(np.arange(length), np.arange(length)) % length
    angles = wrapped * (2.0 * math.pi / length)
    return (np.cos(angles) + np.sin(angles)) / math.sqrt(length)


def constants():
    matrix = jnp.asarray(cas_matrix(SIZE), jnp.float32)
    high = matrix.astype(jnp.bfloat16)
    low = (matrix - high.astype(jnp.float32)).astype(jnp.bfloat16)
    sines = 4.0 * np.sin(np.arange(SIZE) * (math.pi / SIZE)) ** 2
    eigen = (sines[:, None] + sines[None, :]).astype(np.float32)
    eigen = eigen.reshape(SIZE // SUB, SUB, SIZE // LANES, LANES).transpose(0, 2, 1, 3)
    return high, low, jnp.asarray(eigen.reshape(STEPS, SUB, LANES))


def halves(values):
    high = values.astype(jnp.bfloat16)
    return high, (values - high.astype(jnp.float32)).astype(jnp.bfloat16)


def dot(a, b):
    return jnp.dot(a, b, preferred_element_type=jnp.float32)


def dot_right(values, high, low):
    vh, vl = halves(values)
    return dot(vh, high) + (dot(vl, high) + dot(vh, low))


def dot_left(high, low, values):
    vh, vl = halves(values)
    return dot(high, vh) + (dot(high, vl) + dot(low, vh))


def kernel(
    fields, forcing, diffusion, reaction, alpha_ref, mean_ref, shift_ref, high_in, low_in, eigen,
    out, value, source, diff, react, high, low, eig, partner, wrapped, rhs,
    coef, grid, send, recv, in_sems, pair_send, pair_recv, wrap_sems, all_send, all_recv,
):
    group = lax.axis_index("pair")
    place = lax.axis_index("tm")
    loads = [
        pltpu.make_async_copy(src, dst, in_sems.at[i])
        for i, (src, dst) in enumerate(
            (
                (fields, value), (diffusion, diff), (forcing, source), (reaction, react),
                (high_in, high), (low_in, low), (eigen.at[place], eig),
            )
        )
    ]
    for load in loads:
        load.start()

    barrier = pltpu.get_barrier_semaphore()

    def greet(d, c):
        pl.semaphore_signal(
            barrier, inc=1, device_id={"pair": group, "tm": place ^ (STEPS - d)},
            device_id_type=MESH,
        )
        return c

    pl.semaphore_signal(
        barrier, inc=1, device_id={"pair": 1 - group, "tm": place}, device_id_type=MESH
    )
    lax.fori_loop(1, STEPS, greet, 0)

    alpha = alpha_ref[0]
    mean = mean_ref[0]
    shift = shift_ref[0]
    for load in loads:
        load.wait()

    d = diff[...]
    east = 0.5 * (d + pltpu.roll(d, SIZE - 1, 0)) - mean
    north = 0.5 * (d + pltpu.roll(d, SIZE - 1, 1)) - mean
    west = pltpu.roll(east, 1, 0)
    south = pltpu.roll(north, 1, 1)
    coef[0] = east
    coef[1] = west
    coef[2] = north
    coef[3] = south
    coef[4] = shift - ((east + west) + (north + south))

    def linear_part():
        v = value[...]
        total = source[...] + coef[4] * v
        total += coef[0] * pltpu.roll(v, SIZE - 1, 0) + coef[1] * pltpu.roll(v, 1, 0)
        total += coef[2] * pltpu.roll(v, SIZE - 1, 1) + coef[3] * pltpu.roll(v, 1, 1)
        rhs[...] = total

    lam = 1.0 + mean * eig[...] + shift
    ratio = 1.0 / lam
    run_power = ratio
    for _ in range(4):
        run_power = run_power * run_power
    full_power = run_power
    for _ in range(3):
        full_power = full_power * full_power
    wrap_gain = alpha / (1.0 - alpha * full_power)
    last = jnp.zeros_like(ratio)

    linear_part()
    pl.semaphore_wait(barrier, STEPS)

    is_first = place == (STEPS - 1) * group
    is_last = place == (STEPS - 1) * (1 - group)
    wrap_copy = pltpu.make_async_remote_copy(
        src_ref=value, dst_ref=wrapped, send_sem=wrap_sems.at[0], recv_sem=wrap_sems.at[1],
        device_id={"pair": group, "tm": STEPS - 1 - place}, device_id_type=MESH,
    )

    def exchange(phase):
        def one(d, c):
            peer = place ^ (STEPS - d)
            pltpu.make_async_remote_copy(
                src_ref=send.at[phase % 2, peer], dst_ref=recv.at[phase, place],
                send_sem=all_send.at[phase], recv_sem=all_recv.at[phase],
                device_id={"pair": group, "tm": peer}, device_id_type=MESH,
            ).start()
            return c

        lax.fori_loop(1, STEPS, one, 0)
        recv[phase, place] = send[phase % 2, place]

    def exchange_wait(phase):
        span = pl.ds(0, STEPS - 1)
        wait = pltpu.make_async_remote_copy(
            src_ref=send.at[phase % 2, span], dst_ref=recv.at[phase, span],
            send_sem=all_send.at[phase], recv_sem=all_recv.at[phase],
            device_id={"pair": group, "tm": place}, device_id_type=MESH,
        )
        wait.wait_send()
        wait.wait_recv()

    for it in range(ITERS):
        pair_copy = pltpu.make_async_remote_copy(
            src_ref=value, dst_ref=partner.at[it], send_sem=pair_send.at[it],
            recv_sem=pair_recv.at[it], device_id={"pair": 1 - group, "tm": place},
            device_id_type=MESH,
        )
        pair_copy.start()
        if it == 0:

            @pl.when(is_last)
            def _():
                wrap_copy.start()

        if it > 0:
            linear_part()
        v = value[...]
        cubic = react[...] * v
        pair_copy.wait()
        other = partner[it]

        @pl.when(group == 0)
        def _():
            rhs[...] -= cubic * v * v + GAMMA_INV * other

        @pl.when(group == 1)
        def _():
            rhs[...] -= 3.0 * cubic * other * other - other

        if it == 0:

            @pl.when(is_last)
            def _():
                wrap_copy.wait_send()

            @pl.when(is_first)
            def _():
                wrap_copy.wait_recv()
                rhs[...] -= alpha * wrapped[...]

        modes = dot_left(high[...], low[...], dot_right(rhs[...], high[...], low[...]))
        for m in range(STEPS):
            r, c = SUB * (m // 2), LANES * (m % 2)
            send[0, m] = modes[r : r + SUB, c : c + LANES]
        exchange(2 * it)
        exchange_wait(2 * it)

        def slot(i):
            return i + group * (STEPS - 1 - 2 * i)

        runs = STEPS // RUN
        state = [jnp.zeros_like(ratio) for _ in range(runs)]
        for j in range(RUN):
            for b in range(runs):
                n = slot(b * RUN + j)
                state[b] = ratio * (state[b] + recv[2 * it, n])
                send[1, n] = state[b]
        ends = [state[0]]
        for b in range(1, runs):
            ends.append(state[b] + run_power * ends[-1])
        carry = wrap_gain * (ends[-1] - last)
        last = ends[-1] + full_power * carry
        carries = [carry]
        for b in range(1, runs):
            carry = run_power * carry
            carries.append(ends[b - 1] + carry)
        for j in range(RUN):
            for b in range(runs):
                n = slot(b * RUN + j)
                carries[b] = ratio * carries[b]
                send[1, n] += carries[b]
        exchange(2 * it + 1)
        exchange_wait(2 * it + 1)
        for r in range(SIZE // 8):
            for c in range(SIZE // LANES):
                grid[8 * r : 8 * r + 8, LANES * c : LANES * c + LANES] = jnp.concatenate(
                    [recv[2 * it + 1, 4 * r + c], recv[2 * it + 1, 4 * r + 2 + c]], 0
                )
        result = dot_left(high[...], low[...], dot_right(grid[...], high[...], low[...]))
        if it == ITERS - 1:
            out[...] = result
        else:
            value[...] = result


def on_device(fields, forcing, diffusion, reaction, wrap_factor, mean_diffusion, spectral_shift):
    high, low, eigen = constants()
    any_space = pl.BlockSpec(memory_space=pl.ANY)
    scalar = pl.BlockSpec(memory_space=pltpu.SMEM)
    full = (SIZE, SIZE)
    block = (STEPS, SUB, LANES)
    result = pl.pallas_call(
        kernel,
        out_shape=jax.ShapeDtypeStruct(full, jnp.float32),
        in_specs=[any_space] * 4 + [scalar] * 3 + [any_space] * 3,
        out_specs=pl.BlockSpec(memory_space=pltpu.VMEM),
        scratch_shapes=[
            pltpu.VMEM(full, jnp.float32),
            pltpu.VMEM(full, jnp.float32),
            pltpu.VMEM(full, jnp.float32),
            pltpu.VMEM(full, jnp.float32),
            pltpu.VMEM(full, jnp.bfloat16),
            pltpu.VMEM(full, jnp.bfloat16),
            pltpu.VMEM((SUB, LANES), jnp.float32),
            pltpu.VMEM((ITERS,) + full, jnp.float32),
            pltpu.VMEM(full, jnp.float32),
            pltpu.VMEM(full, jnp.float32),
            pltpu.VMEM((5,) + full, jnp.float32),
            pltpu.VMEM(full, jnp.float32),
            pltpu.VMEM((2,) + block, jnp.float32),
            pltpu.VMEM((2 * ITERS,) + block, jnp.float32),
            pltpu.SemaphoreType.DMA((7,)),
            pltpu.SemaphoreType.DMA((ITERS,)),
            pltpu.SemaphoreType.DMA((ITERS,)),
            pltpu.SemaphoreType.DMA((2,)),
            pltpu.SemaphoreType.DMA((2 * ITERS,)),
            pltpu.SemaphoreType.DMA((2 * ITERS,)),
        ],
        compiler_params=pltpu.CompilerParams(
            collective_id=0, has_side_effects=True, vmem_limit_bytes=48 * 1024 * 1024
        ),
    )(
        fields.reshape(full), forcing.reshape(full), diffusion, reaction,
        wrap_factor, mean_diffusion, spectral_shift, high, low, eigen,
    )
    return result[None, None]


def solution(mesh):
    split = P("pair", "tm", None, None)
    return jax.shard_map(
        on_device,
        mesh=mesh,
        in_specs=(split, split, P(), P(), P(), P(), P()),
        out_specs=split,
        check_vma=False,
    )
```

```python
import math

import jax
import jax.numpy as jnp
import numpy as np
from jax import lax
from jax.experimental import pallas as pl
from jax.experimental.pallas import tpu as pltpu
from jax.sharding import PartitionSpec as P

ITERS = 2
GAMMA_INV = 0.5
SIZE = 256
STEPS = 128
CHIPS = 64
HALF = 128
SUB = 4
LANES = 128
RUN = 8
MESH = pl.DeviceIdType.MESH


def cas_matrix(length):
    wrapped = np.outer(np.arange(length), np.arange(length)) % length
    angles = wrapped * (2.0 * math.pi / length)
    return (np.cos(angles) + np.sin(angles)) / math.sqrt(length)


def constants():
    matrix = jnp.asarray(cas_matrix(SIZE), jnp.float32)
    high = matrix.astype(jnp.bfloat16)
    low = (matrix - high.astype(jnp.float32)).astype(jnp.bfloat16)
    sines = 4.0 * np.sin(np.arange(SIZE) * (math.pi / SIZE)) ** 2
    eigen = (sines[:, None] + sines[None, :]).astype(np.float32)
    bands = eigen.reshape(SIZE // SUB, SUB, SIZE // LANES, LANES).transpose(0, 2, 1, 3)
    return high, low, jnp.asarray(eigen), jnp.asarray(bands.reshape(2 * CHIPS, SUB, LANES))


def halves(values):
    high = values.astype(jnp.bfloat16)
    return high, (values - high.astype(jnp.float32)).astype(jnp.bfloat16)


def dot(a, b):
    return jnp.dot(a, b, preferred_element_type=jnp.float32)


def dot_right(values, high, low):
    vh, vl = halves(values)
    return dot(vh, high) + (dot(vl, high) + dot(vh, low))


def dot_left(high, low, values):
    vh, vl = halves(values)
    return dot(high, vh) + (dot(high, vl) + dot(low, vh))


def kernel(
    fields, forcing, diffusion, reaction, alpha_ref, mean_ref, shift_ref, high_in, low_in, eigen,
    bands, out, value, source, diff, react, high, low, eig, ratio_half, partner, wrapped, rhs,
    coef, modes, swap, full, send, recv, in_sems, pair_send, pair_recv, wrap_sems, swap_send,
    swap_recv, all_send, all_recv,
):
    group = lax.axis_index("pair")
    place = lax.axis_index("tm")
    chip = place // 2
    core = place % 2
    loads = [
        pltpu.make_async_copy(src, dst, in_sems.at[i])
        for i, (src, dst) in enumerate(
            (
                (fields, value), (diffusion, diff), (forcing, source), (reaction, react),
                (high_in, high), (low_in, low), (bands.at[core * CHIPS + chip], eig),
                (eigen.at[pl.ds(pl.multiple_of(core * HALF, HALF), HALF)], ratio_half),
            )
        )
    ]
    for load in loads:
        load.start()

    is_first = place == (STEPS - 1) * group
    is_last = place == (STEPS - 1) * (1 - group)
    is_edge = (place == 0) | (place == STEPS - 1)
    barrier = pltpu.get_barrier_semaphore()

    def greet(pair, tm):
        pl.semaphore_signal(
            barrier, inc=1, device_id={"pair": pair, "tm": tm}, device_id_type=MESH
        )

    @pl.when(is_edge)
    def _():
        greet(group, STEPS - 1 - place)

    for d in range(CHIPS - 1, 0, -1):
        greet(group, place ^ (2 * d))
    greet(1 - group, place)
    greet(group, place ^ 1)

    alpha = alpha_ref[0]
    mean = mean_ref[0]
    shift = shift_ref[0]
    for load in loads:
        load.wait()

    d = diff[...]
    east = 0.5 * (d + pltpu.roll(d, SIZE - 1, 0)) - mean
    north = 0.5 * (d + pltpu.roll(d, SIZE - 1, 1)) - mean
    west = pltpu.roll(east, 1, 0)
    south = pltpu.roll(north, 1, 1)
    coef[0] = east
    coef[1] = west
    coef[2] = north
    coef[3] = south
    coef[4] = shift - ((east + west) + (north + south))

    def linear_part():
        v = value[...]
        total = source[...] + coef[4] * v
        total += coef[0] * pltpu.roll(v, SIZE - 1, 0) + coef[1] * pltpu.roll(v, 1, 0)
        total += coef[2] * pltpu.roll(v, SIZE - 1, 1) + coef[3] * pltpu.roll(v, 1, 1)
        rhs[...] = total

    ratio_half[...] = 1.0 / (1.0 + mean * ratio_half[...] + shift)
    ratio = 1.0 / (1.0 + mean * eig[...] + shift)
    pair_ratio = ratio * ratio
    run_power = pair_ratio
    for _ in range(3):
        run_power = run_power * run_power
    full_power = run_power
    for _ in range(3):
        full_power = full_power * full_power
    wrap_gain = alpha / (1.0 - alpha * full_power)
    last = jnp.zeros_like(ratio)
    own_rows = pl.ds(pl.multiple_of(core * HALF, HALF), HALF)
    other_rows = pl.ds(pl.multiple_of((1 - core) * HALF, HALF), HALF)
    own_first = core == group

    linear_part()
    pl.semaphore_wait(barrier, CHIPS + 1 + is_edge.astype(jnp.int32))

    wrap_copy = pltpu.make_async_remote_copy(
        src_ref=value, dst_ref=wrapped, send_sem=wrap_sems.at[0], recv_sem=wrap_sems.at[1],
        device_id={"pair": group, "tm": STEPS - 1 - place}, device_id_type=MESH,
    )

    def exchange(phase):
        for d in range(CHIPS - 1, 0, -1):
            peer = chip ^ d
            pltpu.make_async_remote_copy(
                src_ref=send.at[phase % 2, peer], dst_ref=recv.at[phase, chip],
                send_sem=all_send.at[phase], recv_sem=all_recv.at[phase],
                device_id={"pair": group, "tm": 2 * peer + core}, device_id_type=MESH,
            ).start()
        recv[phase, chip] = send[phase % 2, chip]

    def exchange_wait(phase):
        span = pl.ds(0, CHIPS - 1)
        wait = pltpu.make_async_remote_copy(
            src_ref=send.at[phase % 2, span], dst_ref=recv.at[phase, span],
            send_sem=all_send.at[phase], recv_sem=all_recv.at[phase],
            device_id={"pair": group, "tm": place ^ 1}, device_id_type=MESH,
        )
        wait.wait_send()
        wait.wait_recv()

    def swap_copy(index, src, dst):
        return pltpu.make_async_remote_copy(
            src_ref=src, dst_ref=dst, send_sem=swap_send.at[index], recv_sem=swap_recv.at[index],
            device_id={"pair": group, "tm": place ^ 1}, device_id_type=MESH,
        )

    def slot(i):
        return i + group * (CHIPS - 1 - 2 * i)

    for it in range(ITERS):
        pair_copy = pltpu.make_async_remote_copy(
            src_ref=value, dst_ref=partner.at[it], send_sem=pair_send.at[it],
            recv_sem=pair_recv.at[it], device_id={"pair": 1 - group, "tm": place},
            device_id_type=MESH,
        )
        pair_copy.start()
        if it == 0:

            @pl.when(is_last)
            def _():
                wrap_copy.start()

        if it > 0:
            linear_part()
        v = value[...]
        cubic = react[...] * v
        pair_copy.wait()
        other = partner[it]

        @pl.when(group == 0)
        def _():
            rhs[...] -= cubic * v * v + GAMMA_INV * other

        @pl.when(group == 1)
        def _():
            rhs[...] -= 3.0 * cubic * other * other - other

        if it == 0:

            @pl.when(is_last)
            def _():
                wrap_copy.wait_send()

            @pl.when(is_first)
            def _():
                wrap_copy.wait_recv()
                rhs[...] -= alpha * wrapped[...]

        modes[...] = dot_left(high[...], low[...], dot_right(rhs[...], high[...], low[...]))
        there = swap_copy(2 * it, modes.at[other_rows], swap.at[2 * it])
        there.start()
        there.wait()
        own, sibling = modes[own_rows], swap[2 * it]
        q = ratio_half[...]
        first = jnp.where(own_first, own, sibling)
        second = jnp.where(own_first, sibling, own)
        joined = q * (q * first + second)
        for m in range(CHIPS):
            r, c = SUB * (m // 2), LANES * (m % 2)
            send[0, m] = joined[r : r + SUB, c : c + LANES]
        exchange(2 * it)
        exchange_wait(2 * it)

        runs = CHIPS // RUN
        state = [jnp.zeros_like(ratio) for _ in range(runs)]
        for j in range(RUN):
            for b in range(runs):
                n = slot(b * RUN + j)
                send[1, n] = state[b]
                state[b] = pair_ratio * state[b] + recv[2 * it, n]
        ends = [state[0]]
        for b in range(1, runs):
            ends.append(state[b] + run_power * ends[-1])
        carry = wrap_gain * (ends[-1] - last)
        last = ends[-1] + full_power * carry
        carries = [carry]
        for b in range(1, runs):
            carry = run_power * carry
            carries.append(ends[b - 1] + carry)
        for j in range(RUN):
            for b in range(runs):
                n = slot(b * RUN + j)
                send[1, n] += carries[b]
                carries[b] = pair_ratio * carries[b]
        exchange(2 * it + 1)
        exchange_wait(2 * it + 1)
        rows = []
        for r in range(HALF // 8):
            parts = [
                jnp.concatenate(
                    [recv[2 * it + 1, 4 * r + c], recv[2 * it + 1, 4 * r + 2 + c]], 0
                )
                for c in range(SIZE // LANES)
            ]
            rows.append(jnp.concatenate(parts, 1))
        carry_in = jnp.concatenate(rows, 0)
        own, sibling = modes[own_rows], swap[2 * it]
        first = q * (carry_in + jnp.where(own_first, own, sibling))
        second = q * (first + jnp.where(own_first, sibling, own))
        full[it, own_rows] = jnp.where(own_first, first, second)
        swap[2 * it + 1] = jnp.where(own_first, second, first)
        back = swap_copy(2 * it + 1, swap.at[2 * it + 1], full.at[it, own_rows])
        back.start()
        back.wait()
        result = dot_left(high[...], low[...], dot_right(full[it], high[...], low[...]))
        if it == ITERS - 1:
            out[...] = result
        else:
            value[...] = result


def on_device(fields, forcing, diffusion, reaction, wrap_factor, mean_diffusion, spectral_shift):
    high, low, eigen, bands = constants()
    any_space = pl.BlockSpec(memory_space=pl.ANY)
    scalar = pl.BlockSpec(memory_space=pltpu.SMEM)
    full = (SIZE, SIZE)
    half = (HALF, SIZE)
    block = (CHIPS, SUB, LANES)
    result = pl.pallas_call(
        kernel,
        out_shape=jax.ShapeDtypeStruct(full, jnp.float32),
        in_specs=[any_space] * 4 + [scalar] * 3 + [any_space] * 4,
        out_specs=pl.BlockSpec(memory_space=pltpu.VMEM),
        scratch_shapes=[
            pltpu.VMEM(full, jnp.float32),
            pltpu.VMEM(full, jnp.float32),
            pltpu.VMEM(full, jnp.float32),
            pltpu.VMEM(full, jnp.float32),
            pltpu.VMEM(full, jnp.bfloat16),
            pltpu.VMEM(full, jnp.bfloat16),
            pltpu.VMEM((SUB, LANES), jnp.float32),
            pltpu.VMEM(half, jnp.float32),
            pltpu.VMEM((ITERS,) + full, jnp.float32),
            pltpu.VMEM(full, jnp.float32),
            pltpu.VMEM(full, jnp.float32),
            pltpu.VMEM((5,) + full, jnp.float32),
            pltpu.VMEM(full, jnp.float32),
            pltpu.VMEM((2 * ITERS,) + half, jnp.float32),
            pltpu.VMEM((ITERS,) + full, jnp.float32),
            pltpu.VMEM((2,) + block, jnp.float32),
            pltpu.VMEM((2 * ITERS,) + block, jnp.float32),
            pltpu.SemaphoreType.DMA((8,)),
            pltpu.SemaphoreType.DMA((ITERS,)),
            pltpu.SemaphoreType.DMA((ITERS,)),
            pltpu.SemaphoreType.DMA((2,)),
            pltpu.SemaphoreType.DMA((2 * ITERS,)),
            pltpu.SemaphoreType.DMA((2 * ITERS,)),
            pltpu.SemaphoreType.DMA((2 * ITERS,)),
            pltpu.SemaphoreType.DMA((2 * ITERS,)),
        ],
        compiler_params=pltpu.CompilerParams(
            collective_id=0, has_side_effects=True, vmem_limit_bytes=67043328
        ),
    )(
        fields.reshape(full), forcing.reshape(full), diffusion, reaction,
        wrap_factor, mean_diffusion, spectral_shift, high, low, eigen, bands,
    )
    return result[None, None]


def solution(mesh):
    split = P("pair", "tm", None, None)
    return jax.shard_map(
        on_device,
        mesh=mesh,
        in_specs=(split, split, P(), P(), P(), P(), P()),
        out_specs=split,
        check_vma=False,
    )
```

```python
import math

import jax
import jax.numpy as jnp
import numpy as np
from jax import lax
from jax.experimental import pallas as pl
from jax.experimental.pallas import tpu as pltpu
from jax.sharding import PartitionSpec as P

ITERS = 2
GAMMA_INV = 0.5
SIZE = 256
STEPS = 128
CHIPS = 64
HALF = 128
SUB = 4
LANES = 128
RUN = 8
MESH = pl.DeviceIdType.MESH


def cas_matrix(length):
    wrapped = np.outer(np.arange(length), np.arange(length)) % length
    angles = wrapped * (2.0 * math.pi / length)
    return (np.cos(angles) + np.sin(angles)) / math.sqrt(length)


def constants():
    matrix = jnp.asarray(cas_matrix(SIZE), jnp.float32)
    high = matrix.astype(jnp.bfloat16)
    low = (matrix - high.astype(jnp.float32)).astype(jnp.bfloat16)
    sines = 4.0 * np.sin(np.arange(SIZE) * (math.pi / SIZE)) ** 2
    eigen = (sines[:, None] + sines[None, :]).astype(np.float32)
    bands = eigen.reshape(SIZE // SUB, SUB, SIZE // LANES, LANES).transpose(0, 2, 1, 3)
    return high, low, jnp.asarray(eigen), jnp.asarray(bands.reshape(2 * CHIPS, SUB, LANES))


def halves(values):
    high = values.astype(jnp.bfloat16)
    return high, (values - high.astype(jnp.float32)).astype(jnp.bfloat16)


def dot(a, b):
    return jnp.dot(a, b, preferred_element_type=jnp.float32)


def dot_right(values, high, low):
    vh, vl = halves(values)
    return dot(vh, high) + (dot(vl, high) + dot(vh, low))


def dot_left(high, low, values):
    vh, vl = halves(values)
    return dot(high, vh) + (dot(high, vl) + dot(low, vh))


def kernel(
    fields, forcing, diffusion, reaction, wrap_in, mean_in, shift_in, high_in, low_in, eigen,
    bands, out, wrap_ref, mean_ref, shift_ref, value, source, diff, react, high, low, eig, ratio,
    gain, partner, wrapped, rhs, coef, modes, sibling, part, part_far, joined, arrived, give,
    carry, in_sems, pair_sems, wrap_sems, part_sems, local_sems, swap_send, swap_recv, out_send,
    out_recv, back_send, back_recv, met,
):
    group = lax.axis_index("pair")
    place = lax.axis_index("tm")
    chip = place // 2
    core = place % 2
    loads = [
        pltpu.make_async_copy(src, dst, in_sems.at[i])
        for i, (src, dst) in enumerate(
            (
                (fields, value), (diffusion, diff), (wrap_in, wrap_ref), (mean_in, mean_ref),
                (shift_in, shift_ref), (forcing, source), (eigen, ratio),
                (bands.at[core * CHIPS + chip], eig), (reaction, react), (high_in, high),
                (low_in, low),
            )
        )
    ]
    for load in loads:
        load.start()

    is_first = place == (STEPS - 1) * group
    is_last = place == (STEPS - 1) * (1 - group)
    is_edge = (place == 0) | (place == STEPS - 1)
    barrier = pltpu.get_barrier_semaphore()

    def greet(pair, tm):
        pl.semaphore_signal(
            barrier, inc=1, device_id={"pair": pair, "tm": tm}, device_id_type=MESH
        )

    @pl.when(is_edge)
    def _():
        greet(group, STEPS - 1 - place)

    def chip_at(move_y, move_x, move_z):
        y = (chip // 32 + move_y) % 2
        x = (chip // 8 + move_x) % 4
        z = (chip + move_z) % 8
        return 2 * (32 * y + 8 * x + z) + core

    along_z = [chip_at(0, 0, move) for move in (1, 7, 2, 6)]
    along_x = [chip_at(0, move, 0) for move in (1, 2, 3)]
    along_y = [chip_at(1, 0, 0)]
    greet(1 - group, place)
    for tm in along_z + along_x + along_y + [place ^ 1]:
        greet(group, tm)
    pl.semaphore_wait(barrier, 10 + is_edge.astype(jnp.int32))

    def remote(src, dst, send_sem, recv_sem, pair, tm):
        return pltpu.make_async_remote_copy(
            src_ref=src, dst_ref=dst, send_sem=send_sem, recv_sem=recv_sem,
            device_id={"pair": pair, "tm": tm}, device_id_type=MESH,
        )

    pair_copy = remote(fields, partner, pair_sems.at[0], pair_sems.at[1], 1 - group, place)
    wrap_copy = remote(
        fields, wrapped, wrap_sems.at[0], wrap_sems.at[1], group, STEPS - 1 - place
    )
    pair_copy.start()

    @pl.when(is_last)
    def _():
        wrap_copy.start()

    for load in loads:
        load.wait()

    for stage, peers in enumerate((along_z, along_x, along_y)):
        for tm in peers:
            pl.semaphore_signal(
                met.at[stage], inc=1, device_id={"pair": group, "tm": tm}, device_id_type=MESH
            )
        pl.semaphore_wait(met.at[stage], len(peers))

    alpha = wrap_ref[0]
    mean = mean_ref[0]
    shift = shift_ref[0]

    d = diff[...]
    east = 0.5 * (d + pltpu.roll(d, SIZE - 1, 0)) - mean
    north = 0.5 * (d + pltpu.roll(d, SIZE - 1, 1)) - mean
    west = pltpu.roll(east, 1, 0)
    south = pltpu.roll(north, 1, 1)
    coef[0] = east
    coef[1] = west
    coef[2] = north
    coef[3] = south
    coef[4] = shift - ((east + west) + (north + south))

    def linear_part():
        v = value[...]
        total = source[...] + coef[4] * v
        total += coef[0] * pltpu.roll(v, SIZE - 1, 0) + coef[1] * pltpu.roll(v, 1, 0)
        total += coef[2] * pltpu.roll(v, SIZE - 1, 1) + coef[3] * pltpu.roll(v, 1, 1)
        rhs[...] = total

    own_first = core == group
    single = 1.0 / (1.0 + mean * ratio[...] + shift)
    ratio[...] = single
    gain[0] = jnp.where(own_first, single, single * single)
    gain[1] = jnp.where(own_first, single * single, single)
    band_ratio = 1.0 / (1.0 + mean * eig[...] + shift)
    pair_ratio = band_ratio * band_ratio
    run_power = pair_ratio
    for _ in range(3):
        run_power = run_power * run_power
    full_power = run_power
    for _ in range(3):
        full_power = full_power * full_power
    wrap_gain = alpha / (1.0 - alpha * full_power)
    last = jnp.zeros_like(band_ratio)
    own_rows = pl.ds(pl.multiple_of(core * HALF, HALF), HALF)

    def band(k, offset):
        rows = pl.ds(pl.multiple_of(offset + SUB * (k // 2), SUB), SUB)
        return rows, pl.ds(pl.multiple_of(LANES * (k % 2), LANES), LANES)

    my_rows, my_lanes = band(chip, core * HALF)

    linear_part()

    def slot(i):
        return i + group * (CHIPS - 1 - 2 * i)

    def couple(other):
        v = value[...]
        cubic = react[...] * v

        @pl.when(group == 0)
        def _():
            rhs[...] -= cubic * v * v + GAMMA_INV * other

        @pl.when(group == 1)
        def _():
            rhs[...] -= 3.0 * cubic * other * other - other

    pair_copy.wait()
    couple(partner[...])

    @pl.when(is_last)
    def _():
        wrap_copy.wait_send()

    @pl.when(is_first)
    def _():
        wrap_copy.wait_recv()
        rhs[...] -= alpha * wrapped[...]

    part_copy = remote(part, part_far, part_sems.at[0], part_sems.at[1], 1 - group, place)

    for it in range(ITERS):
        final = it == ITERS - 1
        modes[it] = dot_left(high[...], low[...], dot_right(rhs[...], high[...], low[...]))
        swap = remote(
            modes.at[it], sibling.at[it], swap_send.at[it, 0], swap_recv.at[it, 0], group,
            place ^ 1,
        )
        swap.start()
        swap.wait()
        near, beside = modes[it, own_rows], sibling[it, own_rows]
        q = ratio[own_rows]
        joined[...] = q * jnp.where(own_first, q * near + beside, q * beside + near)
        for d in range(CHIPS - 1, 0, -1):
            peer = chip ^ d
            rows, lanes = band(peer, 0)
            remote(
                joined.at[rows, lanes], arrived.at[it, chip], out_send.at[it], out_recv.at[it],
                group, place ^ (2 * d),
            ).start()
        rows, lanes = band(chip, 0)
        keep = pltpu.make_async_copy(
            joined.at[rows, lanes], arrived.at[it, chip], local_sems.at[it, 0]
        )
        keep.start()
        near = modes[it]
        part[...] = ratio[...] * jnp.where(own_first, near, near + ratio[...] * sibling[it])
        keep.wait()
        span = pl.ds(0, CHIPS - 1)
        wait = remote(
            give.at[span], arrived.at[it, span], out_send.at[it], out_recv.at[it], group,
            place ^ 1,
        )
        wait.wait_send()
        wait.wait_recv()

        runs = CHIPS // RUN
        state = [jnp.zeros_like(band_ratio) for _ in range(runs)]
        for j in range(RUN):
            for b in range(runs):
                n = slot(b * RUN + j)
                give[n] = state[b]
                state[b] = pair_ratio * state[b] + arrived[it, n]
        ends = [state[0]]
        for b in range(1, runs):
            ends.append(state[b] + run_power * ends[-1])
        enter = wrap_gain * (ends[-1] - last)
        last = ends[-1] + full_power * enter
        enters = [enter]
        for b in range(1, runs):
            enter = run_power * enter
            enters.append(ends[b - 1] + enter)
        for j in range(RUN):
            for b in range(runs):
                n = slot(b * RUN + j)
                give[n] += enters[b]
                enters[b] = pair_ratio * enters[b]

        for d in range(CHIPS - 1, -1, -1):
            peer = chip ^ d
            if not final:
                remote(
                    give.at[peer], carry.at[it, 1, my_rows, my_lanes], back_send.at[it, 1],
                    back_recv.at[it, 1], 1 - group, place ^ (2 * d),
                ).start()
            if d:
                remote(
                    give.at[peer], carry.at[it, 0, my_rows, my_lanes], back_send.at[it, 0],
                    back_recv.at[it, 0], group, place ^ (2 * d),
                ).start()
        keep = pltpu.make_async_copy(
            give.at[chip], carry.at[it, 0, my_rows, my_lanes], local_sems.at[it, 1]
        )
        keep.start()
        keep.wait()
        if not final:
            part_copy.start()
        kinds = 1 if final else 2
        swaps = []
        for kind in range(kinds):
            count = CHIPS - 1 + kind
            wait = remote(
                give.at[pl.ds(0, count)], arrived.at[it, pl.ds(0, count)],
                back_send.at[it, kind], back_recv.at[it, kind], group, place ^ 1,
            )
            wait.wait_send()
            wait.wait_recv()
            swap = remote(
                carry.at[it, kind, own_rows], carry.at[it, kind, own_rows],
                swap_send.at[it, 1 + kind], swap_recv.at[it, 1 + kind], group, place ^ 1,
            )
            swap.start()
            swaps.append(swap)
        swaps[0].wait()
        full = gain[0] * carry[it, 0] + part[...]
        result = dot_left(high[...], low[...], dot_right(full, high[...], low[...]))
        if final:
            out[...] = result
        else:
            value[...] = result
            linear_part()
            swaps[1].wait()
            part_copy.wait()
            full = gain[1] * carry[it, 1] + part_far[...]
            couple(dot_left(high[...], low[...], dot_right(full, high[...], low[...])))


def on_device(fields, forcing, diffusion, reaction, wrap_factor, mean_diffusion, spectral_shift):
    high, low, eigen, bands = constants()
    any_space = pl.BlockSpec(memory_space=pl.ANY)
    full = (SIZE, SIZE)
    half = (HALF, SIZE)
    block = (CHIPS, SUB, LANES)
    f32 = jnp.float32
    result = pl.pallas_call(
        kernel,
        out_shape=jax.ShapeDtypeStruct(full, f32),
        in_specs=[any_space] * 11,
        out_specs=pl.BlockSpec(memory_space=pltpu.VMEM),
        scratch_shapes=[
            pltpu.SMEM((1,), f32),
            pltpu.SMEM((1,), f32),
            pltpu.SMEM((1,), f32),
            pltpu.VMEM(full, f32),
            pltpu.VMEM(full, f32),
            pltpu.VMEM(full, f32),
            pltpu.VMEM(full, f32),
            pltpu.VMEM(full, jnp.bfloat16),
            pltpu.VMEM(full, jnp.bfloat16),
            pltpu.VMEM((SUB, LANES), f32),
            pltpu.VMEM(full, f32),
            pltpu.VMEM((2,) + full, f32),
            pltpu.VMEM(full, f32),
            pltpu.VMEM(full, f32),
            pltpu.VMEM(full, f32),
            pltpu.VMEM((5,) + full, f32),
            pltpu.VMEM((ITERS,) + full, f32),
            pltpu.VMEM((ITERS,) + full, f32),
            pltpu.VMEM(full, f32),
            pltpu.VMEM(full, f32),
            pltpu.VMEM(half, f32),
            pltpu.VMEM((ITERS,) + block, f32),
            pltpu.VMEM(block, f32),
            pltpu.VMEM((ITERS, 2) + full, f32),
            pltpu.SemaphoreType.DMA((11,)),
            pltpu.SemaphoreType.DMA((2,)),
            pltpu.SemaphoreType.DMA((2,)),
            pltpu.SemaphoreType.DMA((2,)),
            pltpu.SemaphoreType.DMA((ITERS, 2)),
            pltpu.SemaphoreType.DMA((ITERS, 3)),
            pltpu.SemaphoreType.DMA((ITERS, 3)),
            pltpu.SemaphoreType.DMA((ITERS,)),
            pltpu.SemaphoreType.DMA((ITERS,)),
            pltpu.SemaphoreType.DMA((ITERS, 2)),
            pltpu.SemaphoreType.DMA((ITERS, 2)),
            pltpu.SemaphoreType.REGULAR((3,)),
        ],
        compiler_params=pltpu.CompilerParams(
            collective_id=0, has_side_effects=True, vmem_limit_bytes=67043328
        ),
    )(
        fields.reshape(full), forcing.reshape(full), diffusion, reaction,
        wrap_factor, mean_diffusion, spectral_shift, high, low, eigen, bands,
    )
    return result[None, None]


def solution(mesh):
    split = P("pair", "tm", None, None)
    return jax.shard_map(
        on_device,
        mesh=mesh,
        in_specs=(split, split, P(), P(), P(), P(), P()),
        out_specs=split,
        check_vma=False,
    )
```

```python
import math

import jax
import jax.numpy as jnp
import numpy as np
from jax import lax
from jax.experimental import pallas as pl
from jax.experimental.pallas import tpu as pltpu
from jax.sharding import PartitionSpec as P

ITERS = 2
GAMMA_INV = 0.5
SIZE = 256
STEPS = 128
CHIPS = 64
HALF = 128
SUB = 4
LANES = 128
RUN = 8
MESH = pl.DeviceIdType.MESH


def cas_matrix(length):
    wrapped = np.outer(np.arange(length), np.arange(length)) % length
    angles = wrapped * (2.0 * math.pi / length)
    return (np.cos(angles) + np.sin(angles)) / math.sqrt(length)


def constants():
    sines = 4.0 * np.sin(np.arange(SIZE) * (math.pi / SIZE)) ** 2
    tables = np.concatenate([cas_matrix(SIZE), sines[:, None] + sines[None, :]])
    return jnp.asarray(tables, jnp.float32)


def halves(values):
    high = values.astype(jnp.bfloat16)
    return high, (values - high.astype(jnp.float32)).astype(jnp.bfloat16)


def dot(a, b):
    return jnp.dot(a, b, preferred_element_type=jnp.float32)


def dot_right(values, high, low):
    vh, vl = halves(values)
    return dot(vh, high) + (dot(vl, high) + dot(vh, low))


def dot_left(high, low, values):
    vh, vl = halves(values)
    return dot(high, vh) + (dot(high, vl) + dot(low, vh))


def kernel(
    fields, forcing, diffusion, reaction, wrap_in, mean_in, shift_in, tables, out, wrap_ref, mean_ref, shift_ref, value, source, diff, react, matrix, high, low, eig, ratio,
    gain, partner, wrapped, rhs, coef, modes, sibling, part, part_far, joined, arrived, give,
    carry, in_sems, pair_sems, wrap_sems, part_sems, local_sems, swap_send, swap_recv, out_send,
    out_recv, back_send, back_recv, met,
):
    group = lax.axis_index("pair")
    place = lax.axis_index("tm")
    chip = place // 2
    core = place % 2

    def band(k, offset):
        rows = pl.ds(pl.multiple_of(offset + SUB * (k // 2), SUB), SUB)
        return rows, pl.ds(pl.multiple_of(LANES * (k % 2), LANES), LANES)

    my_rows, my_lanes = band(chip, core * HALF)
    my_eigen, _ = band(chip, SIZE + core * HALF)
    loads = [
        pltpu.make_async_copy(src, dst, in_sems.at[i])
        for i, (src, dst) in enumerate(
            (
                (fields, value), (diffusion, diff), (wrap_in, wrap_ref), (mean_in, mean_ref),
                (shift_in, shift_ref), (forcing, source),
                (tables.at[pl.ds(SIZE, SIZE)], ratio), (tables.at[my_eigen, my_lanes], eig),
                (reaction, react), (tables.at[pl.ds(0, SIZE)], matrix),
            )
        )
    ]
    for load in loads:
        load.start()

    is_first = place == (STEPS - 1) * group
    is_last = place == (STEPS - 1) * (1 - group)
    is_edge = (place == 0) | (place == STEPS - 1)
    barrier = pltpu.get_barrier_semaphore()

    def greet(pair, tm):
        pl.semaphore_signal(
            barrier, inc=1, device_id={"pair": pair, "tm": tm}, device_id_type=MESH
        )

    @pl.when(is_edge)
    def _():
        greet(group, STEPS - 1 - place)

    def chip_at(move_y, move_x, move_z):
        y = (chip // 32 + move_y) % 2
        x = (chip // 8 + move_x) % 4
        z = (chip + move_z) % 8
        return 2 * (32 * y + 8 * x + z) + core

    along_z = [chip_at(0, 0, move) for move in (1, 7, 2, 6)]
    along_x = [chip_at(0, move, 0) for move in (1, 2, 3)]
    along_y = [chip_at(1, 0, 0)]
    greet(1 - group, place)
    for tm in along_z + along_x + along_y + [place ^ 1]:
        greet(group, tm)
    pl.semaphore_wait(barrier, 10 + is_edge.astype(jnp.int32))

    def remote(src, dst, send_sem, recv_sem, pair, tm):
        return pltpu.make_async_remote_copy(
            src_ref=src, dst_ref=dst, send_sem=send_sem, recv_sem=recv_sem,
            device_id={"pair": pair, "tm": tm}, device_id_type=MESH,
        )

    pair_copy = remote(fields, partner, pair_sems.at[0], pair_sems.at[1], 1 - group, place)
    wrap_copy = remote(
        fields, wrapped, wrap_sems.at[0], wrap_sems.at[1], group, STEPS - 1 - place
    )
    pair_copy.start()

    @pl.when(is_last)
    def _():
        wrap_copy.start()

    for load in loads:
        load.wait()

    for stage, peers in enumerate((along_z, along_x, along_y)):
        for tm in peers:
            pl.semaphore_signal(
                met.at[stage], inc=1, device_id={"pair": group, "tm": tm}, device_id_type=MESH
            )
        pl.semaphore_wait(met.at[stage], len(peers))

    alpha = wrap_ref[0]
    mean = mean_ref[0]
    shift = shift_ref[0]

    high[...], low[...] = halves(matrix[...])
    d = diff[...]
    east = 0.5 * (d + pltpu.roll(d, SIZE - 1, 0)) - mean
    north = 0.5 * (d + pltpu.roll(d, SIZE - 1, 1)) - mean
    west = pltpu.roll(east, 1, 0)
    south = pltpu.roll(north, 1, 1)
    coef[0] = east
    coef[1] = west
    coef[2] = north
    coef[3] = south
    coef[4] = shift - ((east + west) + (north + south))

    def linear_part():
        v = value[...]
        total = source[...] + coef[4] * v
        total += coef[0] * pltpu.roll(v, SIZE - 1, 0) + coef[1] * pltpu.roll(v, 1, 0)
        total += coef[2] * pltpu.roll(v, SIZE - 1, 1) + coef[3] * pltpu.roll(v, 1, 1)
        rhs[...] = total

    own_first = core == group
    single = 1.0 / (1.0 + mean * ratio[...] + shift)
    ratio[...] = single
    gain[0] = jnp.where(own_first, single, single * single)
    gain[1] = jnp.where(own_first, single * single, single)
    band_ratio = 1.0 / (1.0 + mean * eig[...] + shift)
    pair_ratio = band_ratio * band_ratio
    run_power = pair_ratio
    for _ in range(3):
        run_power = run_power * run_power
    full_power = run_power
    for _ in range(3):
        full_power = full_power * full_power
    wrap_gain = alpha / (1.0 - alpha * full_power)
    last = jnp.zeros_like(band_ratio)
    own_rows = pl.ds(pl.multiple_of(core * HALF, HALF), HALF)

    other_rows = pl.ds(pl.multiple_of((1 - core) * HALF, HALF), HALF)


    linear_part()

    def slot(i):
        return i + group * (CHIPS - 1 - 2 * i)

    def couple(other):
        v = value[...]
        cubic = react[...] * v

        @pl.when(group == 0)
        def _():
            rhs[...] -= cubic * v * v + GAMMA_INV * other

        @pl.when(group == 1)
        def _():
            rhs[...] -= 3.0 * cubic * other * other - other

    pair_copy.wait()
    couple(partner[...])

    @pl.when(is_last)
    def _():
        wrap_copy.wait_send()

    @pl.when(is_first)
    def _():
        wrap_copy.wait_recv()
        rhs[...] -= alpha * wrapped[...]

    part_copy = remote(part, part_far, part_sems.at[0], part_sems.at[1], 1 - group, place)

    for it in range(ITERS):
        final = it == ITERS - 1
        turned = dot_right(rhs[...], high[...], low[...])
        swaps = []
        for i, rows in enumerate((other_rows, own_rows)):
            modes[it, rows] = dot_left(high[rows], low[rows], turned)
            swaps.append(
                remote(
                    modes.at[it, rows], sibling.at[it, rows], swap_send.at[it, i],
                    swap_recv.at[it, i], group, place ^ 1,
                )
            )
            swaps[-1].start()
        swaps[0].wait()
        near, beside = modes[it, own_rows], sibling[it, own_rows]
        q = ratio[own_rows]
        joined[...] = q * jnp.where(own_first, q * near + beside, q * beside + near)
        for d in range(CHIPS - 1, 0, -1):
            peer = chip ^ d
            rows, lanes = band(peer, 0)
            remote(
                joined.at[rows, lanes], arrived.at[it, chip], out_send.at[it], out_recv.at[it],
                group, place ^ (2 * d),
            ).start()
        rows, lanes = band(chip, 0)
        keep = pltpu.make_async_copy(
            joined.at[rows, lanes], arrived.at[it, chip], local_sems.at[it, 0]
        )
        keep.start()
        swaps[1].wait()
        near = modes[it]
        part[...] = ratio[...] * jnp.where(own_first, near, near + ratio[...] * sibling[it])
        keep.wait()
        span = pl.ds(0, CHIPS - 1)
        wait = remote(
            give.at[span], arrived.at[it, span], out_send.at[it], out_recv.at[it], group,
            place ^ 1,
        )
        wait.wait_send()
        wait.wait_recv()

        runs = CHIPS // RUN
        state = [jnp.zeros_like(band_ratio) for _ in range(runs)]
        for j in range(RUN):
            for b in range(runs):
                n = slot(b * RUN + j)
                give[n] = state[b]
                state[b] = pair_ratio * state[b] + arrived[it, n]
        ends = [state[0]]
        for b in range(1, runs):
            ends.append(state[b] + run_power * ends[-1])
        enter = wrap_gain * (ends[-1] - last)
        last = ends[-1] + full_power * enter
        enters = [enter]
        for b in range(1, runs):
            enter = run_power * enter
            enters.append(ends[b - 1] + enter)
        for j in range(RUN):
            for b in range(runs):
                n = slot(b * RUN + j)
                give[n] += enters[b]
                enters[b] = pair_ratio * enters[b]

        for d in range(CHIPS - 1, -1, -1):
            peer = chip ^ d
            if not final:
                remote(
                    give.at[peer], carry.at[it, 1, my_rows, my_lanes], back_send.at[it, 1],
                    back_recv.at[it, 1], 1 - group, place ^ (2 * d),
                ).start()
            if d:
                remote(
                    give.at[peer], carry.at[it, 0, my_rows, my_lanes], back_send.at[it, 0],
                    back_recv.at[it, 0], group, place ^ (2 * d),
                ).start()
        keep = pltpu.make_async_copy(
            give.at[chip], carry.at[it, 0, my_rows, my_lanes], local_sems.at[it, 1]
        )
        keep.start()
        keep.wait()
        if not final:
            part_copy.start()
        kinds = 1 if final else 2
        swaps = []
        for kind in range(kinds):
            count = CHIPS - 1 + kind
            wait = remote(
                give.at[pl.ds(0, count)], arrived.at[it, pl.ds(0, count)],
                back_send.at[it, kind], back_recv.at[it, kind], group, place ^ 1,
            )
            wait.wait_send()
            wait.wait_recv()
            swap = remote(
                carry.at[it, kind, own_rows], carry.at[it, kind, own_rows],
                swap_send.at[it, 2 + kind], swap_recv.at[it, 2 + kind], group, place ^ 1,
            )
            swap.start()
            swaps.append(swap)
        swaps[0].wait()
        full = gain[0] * carry[it, 0] + part[...]
        result = dot_left(high[...], low[...], dot_right(full, high[...], low[...]))
        if final:
            out[...] = result
        else:
            value[...] = result
            linear_part()
            swaps[1].wait()
            part_copy.wait()
            full = gain[1] * carry[it, 1] + part_far[...]
            couple(dot_left(high[...], low[...], dot_right(full, high[...], low[...])))


def on_device(fields, forcing, diffusion, reaction, wrap_factor, mean_diffusion, spectral_shift):
    tables = constants()
    any_space = pl.BlockSpec(memory_space=pl.ANY)
    full = (SIZE, SIZE)
    half = (HALF, SIZE)
    block = (CHIPS, SUB, LANES)
    f32 = jnp.float32
    result = pl.pallas_call(
        kernel,
        out_shape=jax.ShapeDtypeStruct(full, f32),
        in_specs=[any_space] * 8,
        out_specs=pl.BlockSpec(memory_space=pltpu.VMEM),
        scratch_shapes=[
            pltpu.SMEM((1,), f32),
            pltpu.SMEM((1,), f32),
            pltpu.SMEM((1,), f32),
            pltpu.VMEM(full, f32),
            pltpu.VMEM(full, f32),
            pltpu.VMEM(full, f32),
            pltpu.VMEM(full, f32),
            pltpu.VMEM(full, f32),
            pltpu.VMEM(full, jnp.bfloat16),
            pltpu.VMEM(full, jnp.bfloat16),
            pltpu.VMEM((SUB, LANES), f32),
            pltpu.VMEM(full, f32),
            pltpu.VMEM((2,) + full, f32),
            pltpu.VMEM(full, f32),
            pltpu.VMEM(full, f32),
            pltpu.VMEM(full, f32),
            pltpu.VMEM((5,) + full, f32),
            pltpu.VMEM((ITERS,) + full, f32),
            pltpu.VMEM((ITERS,) + full, f32),
            pltpu.VMEM(full, f32),
            pltpu.VMEM(full, f32),
            pltpu.VMEM(half, f32),
            pltpu.VMEM((ITERS,) + block, f32),
            pltpu.VMEM(block, f32),
            pltpu.VMEM((ITERS, 2) + full, f32),
            pltpu.SemaphoreType.DMA((10,)),
            pltpu.SemaphoreType.DMA((2,)),
            pltpu.SemaphoreType.DMA((2,)),
            pltpu.SemaphoreType.DMA((2,)),
            pltpu.SemaphoreType.DMA((ITERS, 2)),
            pltpu.SemaphoreType.DMA((ITERS, 4)),
            pltpu.SemaphoreType.DMA((ITERS, 4)),
            pltpu.SemaphoreType.DMA((ITERS,)),
            pltpu.SemaphoreType.DMA((ITERS,)),
            pltpu.SemaphoreType.DMA((ITERS, 2)),
            pltpu.SemaphoreType.DMA((ITERS, 2)),
            pltpu.SemaphoreType.REGULAR((3,)),
        ],
        compiler_params=pltpu.CompilerParams(
            collective_id=0, has_side_effects=True, vmem_limit_bytes=54848 * 1024
        ),
    )(
        fields.reshape(full), forcing.reshape(full), diffusion, reaction,
        wrap_factor, mean_diffusion, spectral_shift, tables,
    )
    return result[None, None]


def solution(mesh):
    split = P("pair", "tm", None, None)
    return jax.shard_map(
        on_device,
        mesh=mesh,
        in_specs=(split, split, P(), P(), P(), P(), P()),
        out_specs=split,
        check_vma=False,
    )
```

```python
import math

import jax
import jax.numpy as jnp
import numpy as np
from jax import lax
from jax.experimental import pallas as pl
from jax.experimental.pallas import tpu as pltpu
from jax.sharding import PartitionSpec as P

ITERS = 2
GAMMA_INV = 0.5
SIZE = 256
STEPS = 128
CHIPS = 64
HALF = 128
SUB = 4
LANES = 128
RUN = 8
MESH = pl.DeviceIdType.MESH


def cas_matrix(length):
    wrapped = np.outer(np.arange(length), np.arange(length)) % length
    angles = wrapped * (2.0 * math.pi / length)
    return (np.cos(angles) + np.sin(angles)) / math.sqrt(length)


def constants():
    sines = 4.0 * np.sin(np.arange(SIZE) * (math.pi / SIZE)) ** 2
    tables = np.concatenate([cas_matrix(SIZE), sines[:, None] + sines[None, :]])
    return jnp.asarray(tables, jnp.float32)


def halves(values):
    high = values.astype(jnp.bfloat16)
    return high, (values - high.astype(jnp.float32)).astype(jnp.bfloat16)


def dot(a, b):
    return jnp.dot(a, b, preferred_element_type=jnp.float32)


def dot_right(values, high, low):
    vh, vl = halves(values)
    return dot(vh, high) + (dot(vl, high) + dot(vh, low))


def dot_left(high, low, values):
    vh, vl = halves(values)
    return dot(high, vh) + (dot(high, vl) + dot(low, vh))


def kernel(
    fields, forcing, diffusion, reaction, wrap_in, mean_in, shift_in, tables, out, wrap_ref, mean_ref, shift_ref, value, source, diff, react, matrix, high, low, eig, ratio,
    gain, partner, wrapped, rhs, coef, modes, sibling, part, part_far, joined, arrived, give, seed,
    carry, in_sems, pair_sems, wrap_sems, seed_sems, part_sems, local_sems, swap_send, swap_recv, out_send,
    out_recv, back_send, back_recv, met,
):
    group = lax.axis_index("pair")
    place = lax.axis_index("tm")
    chip = place // 2
    core = place % 2

    def band(k, offset):
        rows = pl.ds(pl.multiple_of(offset + SUB * (k // 2), SUB), SUB)
        return rows, pl.ds(pl.multiple_of(LANES * (k % 2), LANES), LANES)

    my_rows, my_lanes = band(chip, core * HALF)
    my_eigen, _ = band(chip, SIZE + core * HALF)
    loads = [
        pltpu.make_async_copy(src, dst, in_sems.at[i])
        for i, (src, dst) in enumerate(
            (
                (fields, value), (diffusion, diff), (wrap_in, wrap_ref), (mean_in, mean_ref),
                (shift_in, shift_ref), (forcing, source),
                (tables.at[pl.ds(SIZE, SIZE)], ratio), (tables.at[my_eigen, my_lanes], eig),
                (reaction, react), (tables.at[pl.ds(0, SIZE)], matrix),
            )
        )
    ]
    for load in loads:
        load.start()

    is_last = place == (STEPS - 1) * (1 - group)
    is_beside = (place ^ 1) == (STEPS - 1) * (1 - group)
    barrier = pltpu.get_barrier_semaphore()

    def greet(pair, tm):
        pl.semaphore_signal(
            barrier, inc=1, device_id={"pair": pair, "tm": tm}, device_id_type=MESH
        )

    def chip_at(move_y, move_x, move_z):
        y = (chip // 32 + move_y) % 2
        x = (chip // 8 + move_x) % 4
        z = (chip + move_z) % 8
        return 2 * (32 * y + 8 * x + z) + core

    along_z = [chip_at(0, 0, move) for move in (1, 7, 2, 6)]
    along_x = [chip_at(0, move, 0) for move in (1, 2, 3)]
    along_y = [chip_at(1, 0, 0)]
    greet(1 - group, place)
    for tm in along_z + along_x + along_y + [place ^ 1]:
        greet(group, tm)
    pl.semaphore_wait(barrier, 10)

    def remote(src, dst, send_sem, recv_sem, pair, tm):
        return pltpu.make_async_remote_copy(
            src_ref=src, dst_ref=dst, send_sem=send_sem, recv_sem=recv_sem,
            device_id={"pair": pair, "tm": tm}, device_id_type=MESH,
        )

    pair_copy = remote(fields, partner, pair_sems.at[0], pair_sems.at[1], 1 - group, place)
    pair_copy.start()

    for load in loads:
        load.wait()

    for stage, peers in enumerate((along_z, along_x, along_y)):
        for tm in peers:
            pl.semaphore_signal(
                met.at[stage], inc=1, device_id={"pair": group, "tm": tm}, device_id_type=MESH
            )
        pl.semaphore_wait(met.at[stage], len(peers))

    alpha = wrap_ref[0]
    mean = mean_ref[0]
    shift = shift_ref[0]

    high[...], low[...] = halves(matrix[...])
    d = diff[...]
    east = 0.5 * (d + pltpu.roll(d, SIZE - 1, 0)) - mean
    north = 0.5 * (d + pltpu.roll(d, SIZE - 1, 1)) - mean
    west = pltpu.roll(east, 1, 0)
    south = pltpu.roll(north, 1, 1)
    coef[0] = east
    coef[1] = west
    coef[2] = north
    coef[3] = south
    coef[4] = shift - ((east + west) + (north + south))

    def linear_part():
        v = value[...]
        total = source[...] + coef[4] * v
        total += coef[0] * pltpu.roll(v, SIZE - 1, 0) + coef[1] * pltpu.roll(v, 1, 0)
        total += coef[2] * pltpu.roll(v, SIZE - 1, 1) + coef[3] * pltpu.roll(v, 1, 1)
        rhs[...] = total

    own_first = core == group
    single = 1.0 / (1.0 + mean * ratio[...] + shift)
    ratio[...] = single
    gain[0] = jnp.where(own_first, single, single * single)
    gain[1] = jnp.where(own_first, single * single, single)
    band_ratio = 1.0 / (1.0 + mean * eig[...] + shift)
    pair_ratio = band_ratio * band_ratio
    run_power = pair_ratio
    for _ in range(3):
        run_power = run_power * run_power
    full_power = run_power
    for _ in range(3):
        full_power = full_power * full_power
    wrap_gain = alpha / (1.0 - alpha * full_power)
    own_rows = pl.ds(pl.multiple_of(core * HALF, HALF), HALF)

    other_rows = pl.ds(pl.multiple_of((1 - core) * HALF, HALF), HALF)


    linear_part()

    def slot(i):
        return i + group * (CHIPS - 1 - 2 * i)

    def couple(other):
        v = value[...]
        cubic = react[...] * v

        @pl.when(group == 0)
        def _():
            rhs[...] -= cubic * v * v + GAMMA_INV * other

        @pl.when(group == 1)
        def _():
            rhs[...] -= 3.0 * cubic * other * other - other

    wrap_copy = remote(
        wrapped.at[other_rows], wrapped.at[other_rows], wrap_sems.at[0], wrap_sems.at[1], group,
        place ^ 1,
    )
    seed_copies = [
        remote(
            wrapped.at[band(chip ^ d, core * HALF)], seed, seed_sems.at[0], seed_sems.at[1],
            group, place ^ (2 * d),
        )
        for d in range(CHIPS - 1, 0, -1)
    ]

    @pl.when(is_last)
    def _():
        wrapped[...] = dot_left(
            high[...], low[...], dot_right(value[...], high[...], low[...])
        )
        wrap_copy.start()

    @pl.when(is_beside)
    def _():
        wrap_copy.wait_recv()

    @pl.when(is_last | is_beside)
    def _():
        for copy in seed_copies:
            copy.start()
        keep = pltpu.make_async_copy(
            wrapped.at[my_rows, my_lanes], seed, seed_sems.at[2]
        )
        keep.start()
        keep.wait()

    pair_copy.wait()
    couple(partner[...])

    part_copy = remote(part, part_far, part_sems.at[0], part_sems.at[1], 1 - group, place)

    for it in range(ITERS):
        final = it == ITERS - 1
        turned = dot_right(rhs[...], high[...], low[...])
        swaps = []
        for i, rows in enumerate((other_rows, own_rows)):
            modes[it, rows] = dot_left(high[rows], low[rows], turned)
            swaps.append(
                remote(
                    modes.at[it, rows], sibling.at[it, rows], swap_send.at[it, i],
                    swap_recv.at[it, i], group, place ^ 1,
                )
            )
            swaps[-1].start()
        swaps[0].wait()
        near, beside = modes[it, own_rows], sibling[it, own_rows]
        q = ratio[own_rows]
        joined[...] = q * jnp.where(own_first, q * near + beside, q * beside + near)
        for d in range(CHIPS - 1, 0, -1):
            peer = chip ^ d
            rows, lanes = band(peer, 0)
            remote(
                joined.at[rows, lanes], arrived.at[it, chip], out_send.at[it], out_recv.at[it],
                group, place ^ (2 * d),
            ).start()
        rows, lanes = band(chip, 0)
        keep = pltpu.make_async_copy(
            joined.at[rows, lanes], arrived.at[it, chip], local_sems.at[it, 0]
        )
        keep.start()
        swaps[1].wait()
        near = modes[it]
        part[...] = ratio[...] * jnp.where(own_first, near, near + ratio[...] * sibling[it])
        keep.wait()
        span = pl.ds(0, CHIPS - 1)
        wait = remote(
            give.at[span], arrived.at[it, span], out_send.at[it], out_recv.at[it], group,
            place ^ 1,
        )
        wait.wait_send()
        wait.wait_recv()

        if it == 0:

            @pl.when(is_last)
            def _():
                wrap_copy.wait_send()

            @pl.when(is_last | is_beside)
            def _():
                remote(
                    give.at[span], arrived.at[it, span], seed_sems.at[0], seed_sems.at[1], group,
                    place ^ 1,
                ).wait_send()

            @pl.when(jnp.logical_not(is_last | is_beside))
            def _():
                seed_copies[0].wait_recv()

            last = seed[...]

        runs = CHIPS // RUN
        state = [jnp.zeros_like(band_ratio) for _ in range(runs)]
        for j in range(RUN):
            for b in range(runs):
                n = slot(b * RUN + j)
                give[n] = state[b]
                state[b] = pair_ratio * state[b] + arrived[it, n]
        ends = [state[0]]
        for b in range(1, runs):
            ends.append(state[b] + run_power * ends[-1])
        enter = wrap_gain * (ends[-1] - last)
        last = ends[-1] + full_power * enter
        enters = [enter]
        for b in range(1, runs):
            enter = run_power * enter
            enters.append(ends[b - 1] + enter)
        for j in range(RUN):
            for b in range(runs):
                n = slot(b * RUN + j)
                give[n] += enters[b]
                enters[b] = pair_ratio * enters[b]

        for d in range(CHIPS - 1, -1, -1):
            peer = chip ^ d
            if not final:
                remote(
                    give.at[peer], carry.at[it, 1, my_rows, my_lanes], back_send.at[it, 1],
                    back_recv.at[it, 1], 1 - group, place ^ (2 * d),
                ).start()
            if d:
                remote(
                    give.at[peer], carry.at[it, 0, my_rows, my_lanes], back_send.at[it, 0],
                    back_recv.at[it, 0], group, place ^ (2 * d),
                ).start()
        keep = pltpu.make_async_copy(
            give.at[chip], carry.at[it, 0, my_rows, my_lanes], local_sems.at[it, 1]
        )
        keep.start()
        keep.wait()
        if not final:
            part_copy.start()
        kinds = 1 if final else 2
        swaps = []
        for kind in range(kinds):
            count = CHIPS - 1 + kind
            wait = remote(
                give.at[pl.ds(0, count)], arrived.at[it, pl.ds(0, count)],
                back_send.at[it, kind], back_recv.at[it, kind], group, place ^ 1,
            )
            wait.wait_send()
            wait.wait_recv()
            swap = remote(
                carry.at[it, kind, own_rows], carry.at[it, kind, own_rows],
                swap_send.at[it, 2 + kind], swap_recv.at[it, 2 + kind], group, place ^ 1,
            )
            swap.start()
            swaps.append(swap)
        swaps[0].wait()
        full = gain[0] * carry[it, 0] + part[...]
        result = dot_left(high[...], low[...], dot_right(full, high[...], low[...]))
        if final:
            out[...] = result
        else:
            value[...] = result
            linear_part()
            swaps[1].wait()
            part_copy.wait()
            full = gain[1] * carry[it, 1] + part_far[...]
            couple(dot_left(high[...], low[...], dot_right(full, high[...], low[...])))


def on_device(fields, forcing, diffusion, reaction, wrap_factor, mean_diffusion, spectral_shift):
    tables = constants()
    any_space = pl.BlockSpec(memory_space=pl.ANY)
    full = (SIZE, SIZE)
    half = (HALF, SIZE)
    block = (CHIPS, SUB, LANES)
    f32 = jnp.float32
    result = pl.pallas_call(
        kernel,
        out_shape=jax.ShapeDtypeStruct(full, f32),
        in_specs=[any_space] * 8,
        out_specs=pl.BlockSpec(memory_space=pltpu.VMEM),
        scratch_shapes=[
            pltpu.SMEM((1,), f32),
            pltpu.SMEM((1,), f32),
            pltpu.SMEM((1,), f32),
            pltpu.VMEM(full, f32),
            pltpu.VMEM(full, f32),
            pltpu.VMEM(full, f32),
            pltpu.VMEM(full, f32),
            pltpu.VMEM(full, f32),
            pltpu.VMEM(full, jnp.bfloat16),
            pltpu.VMEM(full, jnp.bfloat16),
            pltpu.VMEM((SUB, LANES), f32),
            pltpu.VMEM(full, f32),
            pltpu.VMEM((2,) + full, f32),
            pltpu.VMEM(full, f32),
            pltpu.VMEM(full, f32),
            pltpu.VMEM(full, f32),
            pltpu.VMEM((5,) + full, f32),
            pltpu.VMEM((ITERS,) + full, f32),
            pltpu.VMEM((ITERS,) + full, f32),
            pltpu.VMEM(full, f32),
            pltpu.VMEM(full, f32),
            pltpu.VMEM(half, f32),
            pltpu.VMEM((ITERS,) + block, f32),
            pltpu.VMEM(block, f32),
            pltpu.VMEM((SUB, LANES), f32),
            pltpu.VMEM((ITERS, 2) + full, f32),
            pltpu.SemaphoreType.DMA((10,)),
            pltpu.SemaphoreType.DMA((2,)),
            pltpu.SemaphoreType.DMA((2,)),
            pltpu.SemaphoreType.DMA((3,)),
            pltpu.SemaphoreType.DMA((2,)),
            pltpu.SemaphoreType.DMA((ITERS, 2)),
            pltpu.SemaphoreType.DMA((ITERS, 4)),
            pltpu.SemaphoreType.DMA((ITERS, 4)),
            pltpu.SemaphoreType.DMA((ITERS,)),
            pltpu.SemaphoreType.DMA((ITERS,)),
            pltpu.SemaphoreType.DMA((ITERS, 2)),
            pltpu.SemaphoreType.DMA((ITERS, 2)),
            pltpu.SemaphoreType.REGULAR((3,)),
        ],
        compiler_params=pltpu.CompilerParams(
            collective_id=0, has_side_effects=True, vmem_limit_bytes=54848 * 1024
        ),
    )(
        fields.reshape(full), forcing.reshape(full), diffusion, reaction,
        wrap_factor, mean_diffusion, spectral_shift, tables,
    )
    return result[None, None]


def solution(mesh):
    split = P("pair", "tm", None, None)
    return jax.shard_map(
        on_device,
        mesh=mesh,
        in_specs=(split, split, P(), P(), P(), P(), P()),
        out_specs=split,
        check_vma=False,
    )
```

```python
import math

import jax
import jax.numpy as jnp
import numpy as np
from jax import lax
from jax.experimental import pallas as pl
from jax.experimental.pallas import tpu as pltpu
from jax.sharding import PartitionSpec as P

ITERS = 2
GAMMA_INV = 0.5
SIZE = 256
STEPS = 128
CHIPS = 64
HALF = 128
SUB = 4
LANES = 128
RUN = 8
MESH = pl.DeviceIdType.MESH


def ring(move, length):
    return min(move, length - move)


def hops(move):
    return move[0] + ring(move[1], 4) + ring(move[2], 8)


MOVES = [(y, x, z) for y in range(2) for x in range(4) for z in range(8)][1:]
MOVES.sort(key=lambda move: (-hops(move), -ring(move[2], 8)))


def cas_matrix(length):
    wrapped = np.outer(np.arange(length), np.arange(length)) % length
    angles = wrapped * (2.0 * math.pi / length)
    return (np.cos(angles) + np.sin(angles)) / math.sqrt(length)


def constants():
    sines = 4.0 * np.sin(np.arange(SIZE) * (math.pi / SIZE)) ** 2
    tables = np.concatenate([cas_matrix(SIZE), sines[:, None] + sines[None, :]])
    return jnp.asarray(tables, jnp.float32)


def halves(values):
    high = values.astype(jnp.bfloat16)
    return high, (values - high.astype(jnp.float32)).astype(jnp.bfloat16)


def dot(a, b):
    return jnp.dot(a, b, preferred_element_type=jnp.float32)


def dot_right(values, high, low):
    vh, vl = halves(values)
    return dot(vh, high) + (dot(vl, high) + dot(vh, low))


def dot_left(high, low, values):
    vh, vl = halves(values)
    return dot(high, vh) + (dot(high, vl) + dot(low, vh))


def kernel(
    fields, forcing, diffusion, reaction, wrap_in, mean_in, shift_in, tables, out, wrap_ref, mean_ref, shift_ref, value, source, diff, react, matrix, high, low, eig, ratio,
    gain, partner, wrapped, rhs, coef, modes, sibling, part, part_far, joined, arrived, give, seed,
    carry, in_sems, pair_sems, wrap_sems, seed_sems, part_sems, local_sems, swap_send, swap_recv, out_send,
    out_recv, back_send, back_recv, met,
):
    group = lax.axis_index("pair")
    place = lax.axis_index("tm")
    chip = place // 2
    core = place % 2

    def band(k, offset):
        rows = pl.ds(pl.multiple_of(offset + SUB * (k // 2), SUB), SUB)
        return rows, pl.ds(pl.multiple_of(LANES * (k % 2), LANES), LANES)

    my_rows, my_lanes = band(chip, core * HALF)
    my_eigen, _ = band(chip, SIZE + core * HALF)
    loads = [
        pltpu.make_async_copy(src, dst, in_sems.at[i])
        for i, (src, dst) in enumerate(
            (
                (fields, value), (diffusion, diff), (wrap_in, wrap_ref), (mean_in, mean_ref),
                (shift_in, shift_ref), (forcing, source),
                (tables.at[pl.ds(SIZE, SIZE)], ratio), (tables.at[my_eigen, my_lanes], eig),
                (reaction, react), (tables.at[pl.ds(0, SIZE)], matrix),
            )
        )
    ]
    for load in loads:
        load.start()

    is_last = place == (STEPS - 1) * (1 - group)
    is_beside = (place ^ 1) == (STEPS - 1) * (1 - group)
    barrier = pltpu.get_barrier_semaphore()

    def greet(pair, tm):
        pl.semaphore_signal(
            barrier, inc=1, device_id={"pair": pair, "tm": tm}, device_id_type=MESH
        )

    def peer_at(move):
        y = (chip // 32 + move[0]) % 2
        x = (chip // 8 + move[1]) % 4
        z = (chip + move[2]) % 8
        return 32 * y + 8 * x + z

    def chip_at(*move):
        return 2 * peer_at(move) + core

    along_z = [chip_at(0, 0, move) for move in (1, 7, 2, 6)]
    along_x = [chip_at(0, move, 0) for move in (1, 2, 3)]
    along_y = [chip_at(1, 0, 0)]
    greet(1 - group, place)
    for tm in along_z + along_x + along_y + [place ^ 1]:
        greet(group, tm)
    pl.semaphore_wait(barrier, 10)

    def remote(src, dst, send_sem, recv_sem, pair, tm):
        return pltpu.make_async_remote_copy(
            src_ref=src, dst_ref=dst, send_sem=send_sem, recv_sem=recv_sem,
            device_id={"pair": pair, "tm": tm}, device_id_type=MESH,
        )

    pair_copy = remote(fields, partner, pair_sems.at[0], pair_sems.at[1], 1 - group, place)
    pair_copy.start()

    for load in loads:
        load.wait()

    for stage, peers in enumerate((along_z, along_x, along_y)):
        for tm in peers:
            pl.semaphore_signal(
                met.at[stage], inc=1, device_id={"pair": group, "tm": tm}, device_id_type=MESH
            )
        pl.semaphore_wait(met.at[stage], len(peers))

    alpha = wrap_ref[0]
    mean = mean_ref[0]
    shift = shift_ref[0]

    high[...], low[...] = halves(matrix[...])
    d = diff[...]
    east = 0.5 * (d + pltpu.roll(d, SIZE - 1, 0)) - mean
    north = 0.5 * (d + pltpu.roll(d, SIZE - 1, 1)) - mean
    west = pltpu.roll(east, 1, 0)
    south = pltpu.roll(north, 1, 1)
    coef[0] = east
    coef[1] = west
    coef[2] = north
    coef[3] = south
    coef[4] = shift - ((east + west) + (north + south))

    def linear_part():
        v = value[...]
        total = source[...] + coef[4] * v
        total += coef[0] * pltpu.roll(v, SIZE - 1, 0) + coef[1] * pltpu.roll(v, 1, 0)
        total += coef[2] * pltpu.roll(v, SIZE - 1, 1) + coef[3] * pltpu.roll(v, 1, 1)
        rhs[...] = total

    own_first = core == group
    single = 1.0 / (1.0 + mean * ratio[...] + shift)
    ratio[...] = single
    gain[0] = jnp.where(own_first, single, single * single)
    gain[1] = jnp.where(own_first, single * single, single)
    band_ratio = 1.0 / (1.0 + mean * eig[...] + shift)
    pair_ratio = band_ratio * band_ratio
    run_power = pair_ratio
    for _ in range(3):
        run_power = run_power * run_power
    full_power = run_power
    for _ in range(3):
        full_power = full_power * full_power
    wrap_gain = alpha / (1.0 - alpha * full_power)
    own_rows = pl.ds(pl.multiple_of(core * HALF, HALF), HALF)

    other_rows = pl.ds(pl.multiple_of((1 - core) * HALF, HALF), HALF)


    linear_part()

    def slot(i):
        return i + group * (CHIPS - 1 - 2 * i)

    def couple(other):
        v = value[...]
        cubic = react[...] * v

        @pl.when(group == 0)
        def _():
            rhs[...] -= cubic * v * v + GAMMA_INV * other

        @pl.when(group == 1)
        def _():
            rhs[...] -= 3.0 * cubic * other * other - other

    wrap_copy = remote(
        wrapped.at[other_rows], wrapped.at[other_rows], wrap_sems.at[0], wrap_sems.at[1], group,
        place ^ 1,
    )
    seed_copies = [
        remote(
            wrapped.at[band(peer_at(move), core * HALF)], seed, seed_sems.at[0],
            seed_sems.at[1], group, chip_at(*move),
        )
        for move in MOVES
    ]

    @pl.when(is_last)
    def _():
        wrapped[...] = dot_left(
            high[...], low[...], dot_right(value[...], high[...], low[...])
        )
        wrap_copy.start()

    @pl.when(is_beside)
    def _():
        wrap_copy.wait_recv()

    @pl.when(is_last | is_beside)
    def _():
        for copy in seed_copies:
            copy.start()
        keep = pltpu.make_async_copy(
            wrapped.at[my_rows, my_lanes], seed, seed_sems.at[2]
        )
        keep.start()
        keep.wait()

    pair_copy.wait()
    couple(partner[...])

    part_copy = remote(part, part_far, part_sems.at[0], part_sems.at[1], 1 - group, place)

    for it in range(ITERS):
        final = it == ITERS - 1
        turned = dot_right(rhs[...], high[...], low[...])
        swaps = []
        for i, rows in enumerate((other_rows, own_rows)):
            modes[it, rows] = dot_left(high[rows], low[rows], turned)
            swaps.append(
                remote(
                    modes.at[it, rows], sibling.at[it, rows], swap_send.at[it, i],
                    swap_recv.at[it, i], group, place ^ 1,
                )
            )
            swaps[-1].start()
        swaps[0].wait()
        near, beside = modes[it, own_rows], sibling[it, own_rows]
        q = ratio[own_rows]
        joined[...] = q * jnp.where(own_first, q * near + beside, q * beside + near)
        for move in MOVES:
            peer = peer_at(move)
            rows, lanes = band(peer, 0)
            remote(
                joined.at[rows, lanes], arrived.at[it, chip], out_send.at[it], out_recv.at[it],
                group, 2 * peer + core,
            ).start()
        rows, lanes = band(chip, 0)
        keep = pltpu.make_async_copy(
            joined.at[rows, lanes], arrived.at[it, chip], local_sems.at[it, 0]
        )
        keep.start()
        swaps[1].wait()
        near = modes[it]
        part[...] = ratio[...] * jnp.where(own_first, near, near + ratio[...] * sibling[it])
        keep.wait()
        span = pl.ds(0, CHIPS - 1)
        wait = remote(
            give.at[span], arrived.at[it, span], out_send.at[it], out_recv.at[it], group,
            place ^ 1,
        )
        wait.wait_send()
        wait.wait_recv()

        if it == 0:

            @pl.when(is_last)
            def _():
                wrap_copy.wait_send()

            @pl.when(is_last | is_beside)
            def _():
                remote(
                    give.at[span], arrived.at[it, span], seed_sems.at[0], seed_sems.at[1], group,
                    place ^ 1,
                ).wait_send()

            @pl.when(jnp.logical_not(is_last | is_beside))
            def _():
                seed_copies[0].wait_recv()

            last = seed[...]

        runs = CHIPS // RUN
        state = [jnp.zeros_like(band_ratio) for _ in range(runs)]
        for j in range(RUN):
            for b in range(runs):
                n = slot(b * RUN + j)
                give[n] = state[b]
                state[b] = pair_ratio * state[b] + arrived[it, n]
        ends = [state[0]]
        for b in range(1, runs):
            ends.append(state[b] + run_power * ends[-1])
        enter = wrap_gain * (ends[-1] - last)
        last = ends[-1] + full_power * enter
        enters = [enter]
        for b in range(1, runs):
            enter = run_power * enter
            enters.append(ends[b - 1] + enter)
        for j in range(RUN):
            for b in range(runs):
                n = slot(b * RUN + j)
                give[n] += enters[b]
                enters[b] = pair_ratio * enters[b]

        for move in MOVES + [(0, 0, 0)]:
            peer = peer_at(move)
            if not final:
                remote(
                    give.at[peer], carry.at[it, 1, my_rows, my_lanes], back_send.at[it, 1],
                    back_recv.at[it, 1], 1 - group, 2 * peer + core,
                ).start()
            if any(move):
                remote(
                    give.at[peer], carry.at[it, 0, my_rows, my_lanes], back_send.at[it, 0],
                    back_recv.at[it, 0], group, 2 * peer + core,
                ).start()
        keep = pltpu.make_async_copy(
            give.at[chip], carry.at[it, 0, my_rows, my_lanes], local_sems.at[it, 1]
        )
        keep.start()
        keep.wait()
        if not final:
            part_copy.start()
        kinds = 1 if final else 2
        swaps = []
        for kind in range(kinds):
            count = CHIPS - 1 + kind
            wait = remote(
                give.at[pl.ds(0, count)], arrived.at[it, pl.ds(0, count)],
                back_send.at[it, kind], back_recv.at[it, kind], group, place ^ 1,
            )
            wait.wait_send()
            wait.wait_recv()
            swap = remote(
                carry.at[it, kind, own_rows], carry.at[it, kind, own_rows],
                swap_send.at[it, 2 + kind], swap_recv.at[it, 2 + kind], group, place ^ 1,
            )
            swap.start()
            swaps.append(swap)
        swaps[0].wait()
        full = gain[0] * carry[it, 0] + part[...]
        result = dot_left(high[...], low[...], dot_right(full, high[...], low[...]))
        if final:
            out[...] = result
        else:
            value[...] = result
            linear_part()
            swaps[1].wait()
            part_copy.wait()
            full = gain[1] * carry[it, 1] + part_far[...]
            couple(dot_left(high[...], low[...], dot_right(full, high[...], low[...])))


def on_device(fields, forcing, diffusion, reaction, wrap_factor, mean_diffusion, spectral_shift):
    tables = constants()
    any_space = pl.BlockSpec(memory_space=pl.ANY)
    full = (SIZE, SIZE)
    half = (HALF, SIZE)
    block = (CHIPS, SUB, LANES)
    f32 = jnp.float32
    result = pl.pallas_call(
        kernel,
        out_shape=jax.ShapeDtypeStruct(full, f32),
        in_specs=[any_space] * 8,
        out_specs=pl.BlockSpec(memory_space=pltpu.VMEM),
        scratch_shapes=[
            pltpu.SMEM((1,), f32),
            pltpu.SMEM((1,), f32),
            pltpu.SMEM((1,), f32),
            pltpu.VMEM(full, f32),
            pltpu.VMEM(full, f32),
            pltpu.VMEM(full, f32),
            pltpu.VMEM(full, f32),
            pltpu.VMEM(full, f32),
            pltpu.VMEM(full, jnp.bfloat16),
            pltpu.VMEM(full, jnp.bfloat16),
            pltpu.VMEM((SUB, LANES), f32),
            pltpu.VMEM(full, f32),
            pltpu.VMEM((2,) + full, f32),
            pltpu.VMEM(full, f32),
            pltpu.VMEM(full, f32),
            pltpu.VMEM(full, f32),
            pltpu.VMEM((5,) + full, f32),
            pltpu.VMEM((ITERS,) + full, f32),
            pltpu.VMEM((ITERS,) + full, f32),
            pltpu.VMEM(full, f32),
            pltpu.VMEM(full, f32),
            pltpu.VMEM(half, f32),
            pltpu.VMEM((ITERS,) + block, f32),
            pltpu.VMEM(block, f32),
            pltpu.VMEM((SUB, LANES), f32),
            pltpu.VMEM((ITERS, 2) + full, f32),
            pltpu.SemaphoreType.DMA((10,)),
            pltpu.SemaphoreType.DMA((2,)),
            pltpu.SemaphoreType.DMA((2,)),
            pltpu.SemaphoreType.DMA((3,)),
            pltpu.SemaphoreType.DMA((2,)),
            pltpu.SemaphoreType.DMA((ITERS, 2)),
            pltpu.SemaphoreType.DMA((ITERS, 4)),
            pltpu.SemaphoreType.DMA((ITERS, 4)),
            pltpu.SemaphoreType.DMA((ITERS,)),
            pltpu.SemaphoreType.DMA((ITERS,)),
            pltpu.SemaphoreType.DMA((ITERS, 2)),
            pltpu.SemaphoreType.DMA((ITERS, 2)),
            pltpu.SemaphoreType.REGULAR((3,)),
        ],
        compiler_params=pltpu.CompilerParams(
            collective_id=0, has_side_effects=True, vmem_limit_bytes=54848 * 1024
        ),
    )(
        fields.reshape(full), forcing.reshape(full), diffusion, reaction,
        wrap_factor, mean_diffusion, spectral_shift, tables,
    )
    return result[None, None]


def solution(mesh):
    split = P("pair", "tm", None, None)
    return jax.shard_map(
        on_device,
        mesh=mesh,
        in_specs=(split, split, P(), P(), P(), P(), P()),
        out_specs=split,
        check_vma=False,
    )
```

```python
import math

import jax
import jax.numpy as jnp
import numpy as np
from jax import lax
from jax.experimental import pallas as pl
from jax.experimental.pallas import tpu as pltpu
from jax.sharding import PartitionSpec as P

ITERS = 2
GAMMA_INV = 0.5
SIZE = 256
STEPS = 128
CHIPS = 64
HALF = 128
SUB = 4
LANES = 128
RUN = 8
MESH = pl.DeviceIdType.MESH


def ring(move, length):
    return min(move, length - move)


def hops(move):
    return move[0] + ring(move[1], 4) + ring(move[2], 8)


MOVES = [(y, x, z) for y in range(2) for x in range(4) for z in range(8)][1:]
MOVES.sort(key=lambda move: (-hops(move), -ring(move[2], 8)))


def cas_matrix(length):
    wrapped = np.outer(np.arange(length), np.arange(length)) % length
    angles = wrapped * (2.0 * math.pi / length)
    return (np.cos(angles) + np.sin(angles)) / math.sqrt(length)


def constants():
    sines = 4.0 * np.sin(np.arange(SIZE) * (math.pi / SIZE)) ** 2
    tables = np.concatenate([cas_matrix(SIZE), sines[:, None] + sines[None, :]])
    return jnp.asarray(tables, jnp.float32)


def halves(values):
    high = values.astype(jnp.bfloat16)
    return high, (values - high.astype(jnp.float32)).astype(jnp.bfloat16)


def dot(a, b):
    return jnp.dot(a, b, preferred_element_type=jnp.float32)


def dot_right(values, high, low):
    vh, vl = halves(values)
    return dot(vh, high) + (dot(vl, high) + dot(vh, low))


def dot_left(high, low, values):
    vh, vl = halves(values)
    return dot(high, vh) + (dot(high, vl) + dot(low, vh))


def kernel(
    fields, forcing, diffusion, reaction, wrap_in, mean_in, shift_in, tables, out, wrap_ref, mean_ref, shift_ref, value, source, diff, react, matrix, high, low, eig, ratio,
    gain, partner, wrapped, rhs, coef, modes, sibling, part, part_far, joined, arrived, give, seed,
    carry, in_sems, pair_sems, wrap_sems, seed_sems, part_sems, local_sems, swap_send, swap_recv, out_send,
    out_recv, back_send, back_recv, met,
):
    group = lax.axis_index("pair")
    place = lax.axis_index("tm")
    chip = place // 2
    core = place % 2

    def band(k, offset):
        rows = pl.ds(pl.multiple_of(offset + SUB * (k // 2), SUB), SUB)
        return rows, pl.ds(pl.multiple_of(LANES * (k % 2), LANES), LANES)

    my_rows, my_lanes = band(chip, core * HALF)
    my_eigen, _ = band(chip, SIZE + core * HALF)
    loads = [
        pltpu.make_async_copy(src, dst, in_sems.at[i])
        for i, (src, dst) in enumerate(
            (
                (fields, value), (diffusion, diff), (wrap_in, wrap_ref), (mean_in, mean_ref),
                (shift_in, shift_ref), (forcing, source),
                (tables.at[pl.ds(SIZE, SIZE)], ratio), (tables.at[my_eigen, my_lanes], eig),
                (reaction, react), (tables.at[pl.ds(0, SIZE)], matrix),
            )
        )
    ]
    for load in loads:
        load.start()

    is_last = place == (STEPS - 1) * (1 - group)
    is_beside = (place ^ 1) == (STEPS - 1) * (1 - group)
    barrier = pltpu.get_barrier_semaphore()

    def greet(pair, tm):
        pl.semaphore_signal(
            barrier, inc=1, device_id={"pair": pair, "tm": tm}, device_id_type=MESH
        )

    def peer_at(move):
        y = (chip // 32 + move[0]) % 2
        x = (chip // 8 + move[1]) % 4
        z = (chip + move[2]) % 8
        return 32 * y + 8 * x + z

    def chip_at(*move):
        return 2 * peer_at(move) + core

    along_z = [chip_at(0, 0, move) for move in (1, 7, 2, 6)]
    along_x = [chip_at(0, move, 0) for move in (1, 2, 3)]
    along_y = [chip_at(1, 0, 0)]
    greet(1 - group, place)
    for tm in along_z + along_x + along_y + [place ^ 1]:
        greet(group, tm)
    pl.semaphore_wait(barrier, 10)

    def remote(src, dst, send_sem, recv_sem, pair, tm):
        return pltpu.make_async_remote_copy(
            src_ref=src, dst_ref=dst, send_sem=send_sem, recv_sem=recv_sem,
            device_id={"pair": pair, "tm": tm}, device_id_type=MESH,
        )

    pair_copy = remote(fields, partner, pair_sems.at[0], pair_sems.at[1], 1 - group, place)
    pair_copy.start()

    for load in loads:
        load.wait()

    for stage, peers in enumerate((along_z, along_x, along_y)):
        for tm in peers:
            pl.semaphore_signal(
                met.at[stage], inc=1, device_id={"pair": group, "tm": tm}, device_id_type=MESH
            )
        pl.semaphore_wait(met.at[stage], len(peers))

    alpha = wrap_ref[0]
    mean = mean_ref[0]
    shift = shift_ref[0]

    high[...], low[...] = halves(matrix[...])
    d = diff[...]
    east = 0.5 * (d + pltpu.roll(d, SIZE - 1, 0)) - mean
    north = 0.5 * (d + pltpu.roll(d, SIZE - 1, 1)) - mean
    west = pltpu.roll(east, 1, 0)
    south = pltpu.roll(north, 1, 1)
    coef[0] = east
    coef[1] = west
    coef[2] = north
    coef[3] = south
    coef[4] = shift - ((east + west) + (north + south))

    def linear_part():
        v = value[...]
        total = source[...] + coef[4] * v
        total += coef[0] * pltpu.roll(v, SIZE - 1, 0) + coef[1] * pltpu.roll(v, 1, 0)
        total += coef[2] * pltpu.roll(v, SIZE - 1, 1) + coef[3] * pltpu.roll(v, 1, 1)
        rhs[...] = total

    own_first = core == group
    single = 1.0 / (1.0 + mean * ratio[...] + shift)
    ratio[...] = single
    gain[0] = jnp.where(own_first, single, single * single)
    gain[1] = jnp.where(own_first, single * single, single)
    band_ratio = 1.0 / (1.0 + mean * eig[...] + shift)
    pair_ratio = band_ratio * band_ratio
    run_power = pair_ratio
    for _ in range(3):
        run_power = run_power * run_power
    full_power = run_power
    for _ in range(3):
        full_power = full_power * full_power
    wrap_gain = alpha / (1.0 - alpha * full_power)
    own_rows = pl.ds(pl.multiple_of(core * HALF, HALF), HALF)

    other_rows = pl.ds(pl.multiple_of((1 - core) * HALF, HALF), HALF)


    linear_part()

    def slot(i):
        return i + group * (CHIPS - 1 - 2 * i)

    def couple(other):
        v = value[...]
        cubic = react[...] * v

        @pl.when(group == 0)
        def _():
            rhs[...] -= cubic * v * v + GAMMA_INV * other

        @pl.when(group == 1)
        def _():
            rhs[...] -= 3.0 * cubic * other * other - other

    wrap_copy = remote(
        wrapped.at[other_rows], wrapped.at[other_rows], wrap_sems.at[0], wrap_sems.at[1], group,
        place ^ 1,
    )
    seed_copies = [
        remote(
            wrapped.at[band(peer_at(move), core * HALF)], seed, seed_sems.at[0],
            seed_sems.at[1], group, chip_at(*move),
        )
        for move in MOVES
    ]

    @pl.when(is_last)
    def _():
        wrapped[...] = dot_left(
            high[...], low[...], dot_right(value[...], high[...], low[...])
        )
        wrap_copy.start()

    @pl.when(is_beside)
    def _():
        wrap_copy.wait_recv()

    @pl.when(is_last | is_beside)
    def _():
        for copy in seed_copies:
            copy.start()
        keep = pltpu.make_async_copy(
            wrapped.at[my_rows, my_lanes], seed, seed_sems.at[2]
        )
        keep.start()
        keep.wait()

    pair_copy.wait()
    couple(partner[...])

    part_copy = remote(part, part_far, part_sems.at[0], part_sems.at[1], 1 - group, place)

    for it in range(ITERS):
        final = it == ITERS - 1
        turned = dot_right(rhs[...], high[...], low[...])
        swaps = []
        for i, rows in enumerate((other_rows, own_rows)):
            modes[it, rows] = dot_left(high[rows], low[rows], turned)
            swaps.append(
                remote(
                    modes.at[it, rows], sibling.at[it, rows], swap_send.at[it, i],
                    swap_recv.at[it, i], group, place ^ 1,
                )
            )
            swaps[-1].start()
        swaps[0].wait()
        near, beside = modes[it, own_rows], sibling[it, own_rows]
        q = ratio[own_rows]
        joined[...] = q * jnp.where(own_first, q * near + beside, q * beside + near)
        for move in MOVES:
            peer = peer_at(move)
            rows, lanes = band(peer, 0)
            remote(
                joined.at[rows, lanes], arrived.at[it, chip], out_send.at[it], out_recv.at[it],
                group, 2 * peer + core,
            ).start()
        rows, lanes = band(chip, 0)
        keep = pltpu.make_async_copy(
            joined.at[rows, lanes], arrived.at[it, chip], local_sems.at[it, 0]
        )
        keep.start()
        swaps[1].wait()
        near = modes[it]
        part[...] = ratio[...] * jnp.where(own_first, near, near + ratio[...] * sibling[it])
        if not final:
            part_copy.start()
        keep.wait()
        span = pl.ds(0, CHIPS - 1)
        wait = remote(
            give.at[span], arrived.at[it, span], out_send.at[it], out_recv.at[it], group,
            place ^ 1,
        )
        wait.wait_send()
        wait.wait_recv()

        if it == 0:

            @pl.when(is_last)
            def _():
                wrap_copy.wait_send()

            @pl.when(is_last | is_beside)
            def _():
                remote(
                    give.at[span], arrived.at[it, span], seed_sems.at[0], seed_sems.at[1], group,
                    place ^ 1,
                ).wait_send()

            @pl.when(jnp.logical_not(is_last | is_beside))
            def _():
                seed_copies[0].wait_recv()

            last = seed[...]

        runs = CHIPS // RUN
        state = [jnp.zeros_like(band_ratio) for _ in range(runs)]
        for j in range(RUN):
            for b in range(runs):
                n = slot(b * RUN + j)
                give[n] = state[b]
                state[b] = pair_ratio * state[b] + arrived[it, n]
        ends = [state[0]]
        for b in range(1, runs):
            ends.append(state[b] + run_power * ends[-1])
        enter = wrap_gain * (ends[-1] - last)
        last = ends[-1] + full_power * enter
        enters = [enter]
        for b in range(1, runs):
            enter = run_power * enter
            enters.append(ends[b - 1] + enter)
        for j in range(RUN):
            for b in range(runs):
                n = slot(b * RUN + j)
                give[n] += enters[b]
                enters[b] = pair_ratio * enters[b]

        for move in MOVES + [(0, 0, 0)]:
            peer = peer_at(move)
            if not final:
                remote(
                    give.at[peer], carry.at[it, 1, my_rows, my_lanes], back_send.at[it, 1],
                    back_recv.at[it, 1], 1 - group, 2 * peer + core,
                ).start()
            if any(move):
                remote(
                    give.at[peer], carry.at[it, 0, my_rows, my_lanes], back_send.at[it, 0],
                    back_recv.at[it, 0], group, 2 * peer + core,
                ).start()
        keep = pltpu.make_async_copy(
            give.at[chip], carry.at[it, 0, my_rows, my_lanes], local_sems.at[it, 1]
        )
        keep.start()
        keep.wait()
        kinds = 1 if final else 2
        swaps = []
        for kind in range(kinds):
            count = CHIPS - 1 + kind
            wait = remote(
                give.at[pl.ds(0, count)], arrived.at[it, pl.ds(0, count)],
                back_send.at[it, kind], back_recv.at[it, kind], group, place ^ 1,
            )
            wait.wait_send()
            wait.wait_recv()
            swap = remote(
                carry.at[it, kind, own_rows], carry.at[it, kind, own_rows],
                swap_send.at[it, 2 + kind], swap_recv.at[it, 2 + kind], group, place ^ 1,
            )
            swap.start()
            swaps.append(swap)
        swaps[0].wait()
        full = gain[0] * carry[it, 0] + part[...]
        result = dot_left(high[...], low[...], dot_right(full, high[...], low[...]))
        if final:
            out[...] = result
        else:
            value[...] = result
            linear_part()
            swaps[1].wait()
            part_copy.wait()
            full = gain[1] * carry[it, 1] + part_far[...]
            couple(dot_left(high[...], low[...], dot_right(full, high[...], low[...])))


def on_device(fields, forcing, diffusion, reaction, wrap_factor, mean_diffusion, spectral_shift):
    tables = constants()
    any_space = pl.BlockSpec(memory_space=pl.ANY)
    full = (SIZE, SIZE)
    half = (HALF, SIZE)
    block = (CHIPS, SUB, LANES)
    f32 = jnp.float32
    result = pl.pallas_call(
        kernel,
        out_shape=jax.ShapeDtypeStruct(full, f32),
        in_specs=[any_space] * 8,
        out_specs=pl.BlockSpec(memory_space=pltpu.VMEM),
        scratch_shapes=[
            pltpu.SMEM((1,), f32),
            pltpu.SMEM((1,), f32),
            pltpu.SMEM((1,), f32),
            pltpu.VMEM(full, f32),
            pltpu.VMEM(full, f32),
            pltpu.VMEM(full, f32),
            pltpu.VMEM(full, f32),
            pltpu.VMEM(full, f32),
            pltpu.VMEM(full, jnp.bfloat16),
            pltpu.VMEM(full, jnp.bfloat16),
            pltpu.VMEM((SUB, LANES), f32),
            pltpu.VMEM(full, f32),
            pltpu.VMEM((2,) + full, f32),
            pltpu.VMEM(full, f32),
            pltpu.VMEM(full, f32),
            pltpu.VMEM(full, f32),
            pltpu.VMEM((5,) + full, f32),
            pltpu.VMEM((ITERS,) + full, f32),
            pltpu.VMEM((ITERS,) + full, f32),
            pltpu.VMEM(full, f32),
            pltpu.VMEM(full, f32),
            pltpu.VMEM(half, f32),
            pltpu.VMEM((ITERS,) + block, f32),
            pltpu.VMEM(block, f32),
            pltpu.VMEM((SUB, LANES), f32),
            pltpu.VMEM((ITERS, 2) + full, f32),
            pltpu.SemaphoreType.DMA((10,)),
            pltpu.SemaphoreType.DMA((2,)),
            pltpu.SemaphoreType.DMA((2,)),
            pltpu.SemaphoreType.DMA((3,)),
            pltpu.SemaphoreType.DMA((2,)),
            pltpu.SemaphoreType.DMA((ITERS, 2)),
            pltpu.SemaphoreType.DMA((ITERS, 4)),
            pltpu.SemaphoreType.DMA((ITERS, 4)),
            pltpu.SemaphoreType.DMA((ITERS,)),
            pltpu.SemaphoreType.DMA((ITERS,)),
            pltpu.SemaphoreType.DMA((ITERS, 2)),
            pltpu.SemaphoreType.DMA((ITERS, 2)),
            pltpu.SemaphoreType.REGULAR((3,)),
        ],
        compiler_params=pltpu.CompilerParams(
            collective_id=0, has_side_effects=True, vmem_limit_bytes=54848 * 1024
        ),
    )(
        fields.reshape(full), forcing.reshape(full), diffusion, reaction,
        wrap_factor, mean_diffusion, spectral_shift, tables,
    )
    return result[None, None]


def solution(mesh):
    split = P("pair", "tm", None, None)
    return jax.shard_map(
        on_device,
        mesh=mesh,
        in_specs=(split, split, P(), P(), P(), P(), P()),
        out_specs=split,
        check_vma=False,
    )
```
